32 devices in a mesh: gx: 8 (over y, x, core), gy: 4 (over z).
Axes of the slice: x: 2, y: 2, z: 4, core: 2. Of those that a mesh axis runs over, the one named last changes fastest.
Arguments:
- wave_coeffs: bfloat16 [768, 131072], P('gy', 'gx'), may hold values from -6 to 6
- projectors: bfloat16 [256, 131072], P(None, 'gx'), may hold values from -0.0234375 to 0.0234375
- miller_index: int32 [3, 131072], P(None, 'gx'), may hold values from -32 to 31, as said below
- occupations: float32 [768], P('gy'), may hold values from 0 to 2
- species_map: int32 [32], replicated, may hold values from 0 to 3
- proj_counts: int32 [32], replicated, may hold values from 1 to 8, as said below
- onsite_base: float32 [4, 8, 8], replicated, may hold values from -5 to 5
Outputs:
- new_bands: float32 [768, 131072], P('gy', 'gx')
The draws below stay inside these ranges and needn't reach their ends.
Inputs may be any that keep to these rules, and one draw needn't show every extreme that they name: `miller_index`: each column is a distinct lattice vector; columns run through whole shells of equal squared length in increasing order, the last shell possibly in part. `proj_counts`: some atom has exactly 8 projectors and some atom exactly one.
All inputs are finite; a program needn't handle non-finite values.
Results may differ from the reference program's by a relative error of at most 0.0031.
Values may be sent and summed in bfloat16 or wider, within the bound.
No kernel may reach another device: no remote copies, remote signals or barrier semaphores. Data moves between devices by JAX's collectives and lax.ppermute only.
A program may use at most 64 MiB of HBM per device.

```python
import math
import jax
import jax.numpy as jnp
import numpy as np
from jax import lax

G = 131072
PMAX = 8
SPECIES = 4
ITERS = 2
BANDS = 768
ATOMS = 32


def draw_miller_index(key, part):
    cube_side = 64
    cube_cells = jnp.arange(cube_side * cube_side * cube_side, dtype=jnp.int32)
    first_axis = cube_cells // (cube_side * cube_side) - 32
    second_axis = cube_cells // cube_side % cube_side - 32
    third_axis = cube_cells % cube_side - 32
    radius_sq = first_axis * first_axis + second_axis * second_axis + third_axis * third_axis
    shuffle = jax.random.permutation(jax.random.fold_in(key, 7), cube_side * cube_side * cube_side).astype(jnp.int32)
    scores = radius_sq * (cube_side * cube_side * cube_side) + shuffle
    sorted_cells = jnp.argsort(scores)[:G]
    return jnp.stack([first_axis[sorted_cells], second_axis[sorted_cells], third_axis[sorted_cells]]).astype(jnp.int32)


def draw_proj_counts(key, part):
    base_draw = jax.random.randint(jax.random.fold_in(key, 3), (ATOMS,), 2, PMAX + 1).astype(jnp.int32)
    placed = jax.random.permutation(jax.random.fold_in(key, 5), ATOMS)
    return base_draw.at[placed[0]].set(PMAX).at[placed[1]].set(1).astype(jnp.int32)


def place_ends(values, rng, smallest, high):
    place = [jax.random.randint(jax.random.fold_in(rng, axis), (), 0, length) for axis, length in enumerate(values.shape)]
    main_axis = values.shape.index(max(values.shape))
    next_to = place[:main_axis] + [(place[main_axis] + 1) % values.shape[main_axis]] + place[main_axis + 1:]
    return values.at[tuple(place)].set(smallest).at[tuple(next_to)].set(high)


def spiked(values, rng, source, target, parts, factor):
    owner, partner = [(jnp.arange(values.shape[axis_at]) // (values.shape[axis_at] // parts)).reshape([-1 if axis == axis_at else 1 for axis in range(values.ndim)]) for axis_at in (source, target)]
    chosen = jax.random.permutation(rng, parts)[partner]
    strong = (owner == chosen) | (owner == (partner + parts // 2) % parts)
    return jnp.where(strong, factor * values, values)


def shard_levels(own_key, extent, shards, smallest, largest):
    level, own = 1.0, jax.random.fold_in(own_key, 6)
    for axis_at, shards_of in shards:
        steps = jnp.exp(jax.random.uniform(jax.random.fold_in(own, axis_at), (shards_of,), jnp.float32, smallest / len(shards), largest / len(shards)))
        level = level * jnp.repeat(steps, extent[axis_at] // shards_of).reshape([-1 if axis == axis_at else 1 for axis in range(len(extent))])
    return level


def rank_bounds(count, slope):
    portions = [(1 << 20) // math.isqrt(standing ** slope) + 1 for standing in range(1, count + 1)]
    spread = 1 + sum(portions) // (1 << 30)
    return np.cumsum(np.array([max(1, weight // spread) for weight in portions]))


def skewed_ids(own_key, dims, count, skew):
    grid = rank_bounds(count, skew)
    lot = jax.random.randint(jax.random.fold_in(own_key, 1), dims, 0, int(grid[count - 1]))
    standing = jnp.searchsorted(jnp.asarray(grid, jnp.int32), lot, side="right")
    return jax.random.permutation(jax.random.fold_in(own_key, 2), count)[standing].astype(jnp.int32)


def scatter_about(key, extent, scale, most, pieces=(), held_as=jnp.bfloat16):
    drawn = jax.random.normal(key, extent, jnp.float32) * scale
    if len(pieces) > 0:
        drawn = shard_levels(key, extent, pieces, -0.22, 0.18) * drawn
    return jnp.clip(drawn, min=-most, max=most).astype(held_as)


def heavy_noise(key, extent, deviation, limit, cuts, heavy, kind=jnp.bfloat16):
    entries = deviation * jax.random.normal(key, extent, jnp.float32)
    if cuts:
        entries = entries * shard_levels(key, extent, cuts, -0.22, 0.18)
    return jnp.clip(spiked(entries, jax.random.fold_in(key, 3), *heavy), -limit, limit).astype(kind)


def setup_inputs(seed: int = 0) -> dict:
    seeds = jax.random.split(jax.random.key(seed), 8)
    return {
        "wave_coeffs": scatter_about(seeds[0], (BANDS, G), 1.0, 6.0, ((0, 4), (1, 8))),
        "projectors": heavy_noise(seeds[1], (ATOMS * PMAX, G), G ** -0.5, 0.0234375, ((1, 8),), (1, 0, 8, 2.0)),
        "miller_index": draw_miller_index(jax.random.fold_in(seeds[7], 71), 0),
        "occupations": jnp.clip(2.0 * jax.random.uniform(seeds[3], (BANDS,), jnp.float32) ** shard_levels(seeds[3], (BANDS,), ((0, 4),), -0.2, 0.2), 0.0, 2.0),
        "species_map": place_ends(skewed_ids(seeds[4], (ATOMS,), SPECIES, 2), jax.random.fold_in(seeds[4], 3), 0, SPECIES - 1).astype(jnp.int32),
        "proj_counts": draw_proj_counts(jax.random.fold_in(seeds[7], 71), 0),
        "onsite_base": scatter_about(seeds[6], (SPECIES, PMAX, PMAX), 1.0, 5.0, (), jnp.float32),
    }


kinetic_unit = 1.0 / 600.0
hubbard_weight = 2.0
step_length = 0.5


def kinetic_of(miller_index):
    components = miller_index.astype(jnp.float32)
    metric = jnp.array([1.5, 1.0, 0.5], dtype=jnp.float32)
    return jnp.sum(metric[:, None] * components * components, axis=0) * kinetic_unit


def teter_factor(kinetic, band_kinetic):
    scaled_kinetic = kinetic[None, :] / band_kinetic[:, None]
    numerator = 27.0 + scaled_kinetic * (18.0 + scaled_kinetic * (12.0 + 8.0 * scaled_kinetic))
    return numerator / (numerator + 16.0 * scaled_kinetic ** 4)


def onsite_apply(raw_proj, occupations, species_map, proj_counts, onsite_base):
    atom_count, slot_width, band_total = raw_proj.shape
    slot_index = jnp.arange(slot_width, dtype=jnp.int32)
    live_slots = (slot_index[None, :] < proj_counts[:, None]).astype(jnp.float32)
    masked = raw_proj * live_slots[:, :, None]
    density = jnp.einsum("apb,aqb->apq", masked * occupations[None, None, :], masked, precision=lax.Precision.HIGHEST) / band_total
    kind_count = onsite_base.shape[0]
    onehot = (species_map[:, None] == jnp.arange(kind_count, dtype=jnp.int32)[None, :]).astype(jnp.float32)
    symmetric = 0.5 * (onsite_base + jnp.swapaxes(onsite_base, 1, 2))
    base_here = jnp.dot(onehot, symmetric.reshape(kind_count, slot_width * slot_width), precision=lax.Precision.HIGHEST).reshape(atom_count, slot_width, slot_width)
    onsite = base_here + hubbard_weight * density
    weighted = jnp.einsum("apq,aqb->apb", onsite, masked, precision=lax.Precision.HIGHEST) * live_slots[:, :, None]
    return masked, weighted


def reference(wave_coeffs, projectors, miller_index, occupations, species_map, proj_counts, onsite_base):
    kinetic = kinetic_of(miller_index)
    current = wave_coeffs
    updated = wave_coeffs.astype(jnp.float32)
    for turn_index in range(ITERS):
        values = current.astype(jnp.float32)
        intersections = lax.dot_general(projectors, current, (((1,), (1,)), ((), ())), preferred_element_type=jnp.float32)
        raw_proj = intersections.reshape(ATOMS, PMAX, BANDS)
        masked, weighted = onsite_apply(raw_proj, occupations, species_map, proj_counts, onsite_base)
        weight_bf = weighted.reshape(ATOMS * PMAX, BANDS).astype(jnp.bfloat16)
        nonlocal_part = lax.dot_general(weight_bf, projectors, (((0,), (0,)), ((), ())), preferred_element_type=jnp.float32)
        applied = kinetic[None, :] * values + nonlocal_part
        norm_sq = jnp.sum(values * values, axis=1)
        kin_sum = jnp.sum(kinetic[None, :] * values * values, axis=1)
        energy_sum = jnp.sum(values * applied, axis=1)
        eigen_value = energy_sum / norm_sq
        band_kinetic = kin_sum / norm_sq
        residual = applied - eigen_value[:, None] * values
        updated = values - step_length * teter_factor(kinetic, band_kinetic) * residual
        if turn_index + 1 < ITERS:
            current = updated.astype(jnp.bfloat16)
    return updated
```

```python
import functools

import jax
import jax.numpy as jnp
from jax import lax
from jax.experimental import pallas as pl
from jax.experimental.pallas import tpu as pltpu
from jax.sharding import PartitionSpec as P

PMAX = 8
ITERS = 2
LANES = 128
ROWS = 16
MIB = 1 << 20
F32 = jnp.float32
BF16 = jnp.bfloat16
HIGH = lax.Precision.HIGHEST


kinetic_unit = 1.0 / 600.0
hubbard_weight = 2.0
step_length = 0.5

NT = (((1,), (1,)), ((), ()))
TN = (((0,), (0,)), ((), ()))


def stat_slots(bands, half):
    return -(-bands // half)


def column_of(rows, first, last):
    pick = lax.broadcasted_iota(jnp.int32, (ROWS, LANES), 0)
    ones = jnp.where((pick >= first) & (pick < last), 1.0, 0.0).astype(F32)
    return lax.dot_general(rows, ones, TN, precision=HIGH, preferred_element_type=F32)


def whole_rows(stats):
    row = lax.broadcasted_iota(jnp.int32, stats.shape, 0)
    return jnp.where(row % 2 == 0, stats + pltpu.roll(stats, ROWS - 1, 0), 0.0)


def split_rows(stats):
    head = stats.astype(BF16).astype(F32)
    rest = pltpu.roll(stats - head, 1, 0)
    row = lax.broadcasted_iota(jnp.int32, stats.shape, 0)
    return jnp.where(row % 2 == 0, head, rest).astype(BF16)


def rows_for(stats, kind):
    return split_rows(stats) if kind == BF16 else stats


def pack_partials(core, acc, stat_acc, own, other):
    bands = acc.shape[0]
    half = own.shape[1]
    kind = other.dtype
    own[0:bands, :] = acc[:, pl.ds(pl.multiple_of(core * half, LANES), half)]
    other[0:bands, :] = acc[:, pl.ds(pl.multiple_of((1 - core) * half, LANES), half)].astype(kind)
    row = lax.broadcasted_iota(jnp.int32, stat_acc.shape, 0)
    stats = whole_rows(jnp.where(row < 2, stat_acc[...], 2.0 * stat_acc[...]))
    split = rows_for(stats, kind)
    for slot in range(stat_slots(bands, half)):
        at = bands + ROWS * slot
        width = min(half, bands - slot * half)
        own[at : at + ROWS, :] = jnp.zeros((ROWS, half), F32)
        other[at : at + ROWS, :] = jnp.zeros((ROWS, half), kind)
        own[at : at + ROWS, 0:width] = stats[:, slot * half : slot * half + width]
        other[at : at + ROWS, 0:width] = split[:, slot * half : slot * half + width]


def first_kernel(
    chunk, core_ref, wave, proj, miller, occ, base, species_hbm, counts_hbm,
    bands_out, proj_out, kin_out, weigh_out, live_out, base_out, occ_out, own, other,
    acc, stat_acc, squares, miller_buf, occ_buf, base_buf, species, counts, sems, small_sems,
):
    core = core_ref[0]
    bands, plane = wave.shape
    steps = plane // chunk
    half = own.shape[1]
    small = [
        pltpu.make_async_copy(source, target, small_sems.at[index])
        for index, (source, target) in enumerate(
            (
                (miller, miller_buf),
                (occ, occ_buf),
                (base, base_buf),
                (species_hbm, species),
                (counts_hbm, counts),
            )
        )
    ]
    for copy in small:
        copy.start()

    def copies(step):
        span = pl.ds(step * chunk, chunk)
        return (
            pltpu.make_async_copy(wave.at[:, span], bands_out.at[:, span], sems.at[0, step]),
            pltpu.make_async_copy(proj.at[:, span], proj_out.at[:, span], sems.at[1, step]),
        )

    for step in range(steps):
        for copy in copies(step):
            copy.start()
    acc[...] = jnp.zeros_like(acc)
    stat_acc[...] = jnp.zeros_like(stat_acc)
    for copy in small:
        copy.wait()

    lane = lax.broadcasted_iota(jnp.int32, (PMAX, half), 1)
    slot = lane % PMAX
    atom = lane // PMAX
    atoms_half = half // PMAX

    def tables(index, held):
        count_row, kind_row = held
        here = atom == index
        source = core * atoms_half + index
        return (
            jnp.where(here, counts[source], count_row),
            jnp.where(here, species[source], kind_row),
        )

    zero = jnp.zeros((PMAX, half), jnp.int32)
    count_row, kind_row = lax.fori_loop(0, atoms_half, tables, (zero, zero))
    live_out[...] = jnp.where(slot < count_row, 1.0, 0.0).astype(F32)
    spread = jnp.where(
        lane == lane // PMAX * PMAX + lax.broadcasted_iota(jnp.int32, (PMAX, half), 0), 1.0, 0.0
    ).astype(F32)
    table = jnp.zeros((PMAX, half), F32)
    for kind in range(base.shape[0]):
        block = base_buf[kind]
        symmetric = 0.5 * (
            lax.dot_general(
                block, spread, (((1,), (0,)), ((), ())), precision=HIGH, preferred_element_type=F32
            )
            + lax.dot_general(block, spread, TN, precision=HIGH, preferred_element_type=F32)
        )
        table = jnp.where(kind_row == kind, symmetric, table)
    base_out[...] = table
    occ_rows = jnp.broadcast_to(occ_buf[...], (ROWS, bands))
    occ_out[...] = column_of(occ_rows, 0, 1)

    def step_body(step, carry):
        span = pl.ds(pl.multiple_of(step * chunk, LANES), chunk)
        parts = miller_buf[:, span].astype(F32)
        m0, m1, m2 = parts[0:1], parts[1:2], parts[2:3]
        kinetic = (1.5 * m0 * m0 + m1 * m1 + 0.5 * m2 * m2) * kinetic_unit
        halved = jnp.broadcast_to(step_length * kinetic, (ROWS, chunk))
        kin_out[:, span] = halved
        head = halved.astype(BF16).astype(F32)
        row = lax.broadcasted_iota(jnp.int32, (ROWS, chunk), 0)
        weigh_out[:, span] = jnp.where(
            row == 0, 1.0, jnp.where(row == 2, head, jnp.where(row == 3, halved - head, 0.0))
        ).astype(BF16)
        for copy in copies(step):
            copy.wait()
        values = bands_out[:, span]
        squares[...] = values * values
        acc[...] += lax.dot_general(
            values, proj_out[:, span], NT, preferred_element_type=F32
        )
        stat_acc[...] += lax.dot_general(
            weigh_out[:, span], squares[...], NT, preferred_element_type=F32
        )
        return carry

    lax.fori_loop(0, steps, step_body, 0)
    pack_partials(core, acc, stat_acc, own, other)


def pair_kernel(own, came, total, sent):
    rows, half = own.shape
    kind = sent.dtype
    value = own[...] + came[...].astype(F32)
    total[...] = value
    sent[...] = value.astype(kind)
    bands = rows - ROWS * stat_slots_of(rows, half)
    if kind == BF16:
        for at in range(bands, rows, ROWS):
            whole = whole_rows(value[at : at + ROWS])
            total[at : at + ROWS, :] = whole
            sent[at : at + ROWS, :] = split_rows(whole)


def stat_slots_of(rows, half):
    slots = 1
    while stat_slots(rows - ROWS * slots, half) != slots:
        slots += 1
    return slots


def density_kernel(count, *refs):
    total, came = refs[0], refs[1 : 1 + count]
    live, occ, masked, density, scale, band_kin, norm_inv, rows_buf = refs[1 + count :]
    rows, half = total.shape
    bands = masked.shape[0]
    value = total[...]
    for ref in came:
        value = value + ref[...].astype(F32)
    kept = value[0:bands] * live[0:1, :]
    masked[...] = kept
    full = lax.dot_general(
        kept * occ_wide(occ, half), kept, TN, precision=HIGH, preferred_element_type=F32
    )
    atom = lax.broadcasted_iota(jnp.int32, (PMAX, half), 1) // PMAX
    compact = jnp.zeros((PMAX, half), F32)
    for index in range(half // PMAX):
        block = full[index * PMAX : (index + 1) * PMAX]
        compact = jnp.where(atom == index, block, compact)
    density[...] = compact
    for slot in range(stat_slots(bands, half)):
        at = bands + ROWS * slot
        width = min(half, bands - slot * half)
        rows_buf[:, slot * half : slot * half + width] = value[at : at + ROWS, 0:width]
    norm = column_of(rows_buf[...], 0, 2)
    kin = column_of(rows_buf[...], 2, 4)
    mean = kin / norm
    band_kin[...] = mean
    norm_inv[...] = 1.0 / norm
    scale[...] = 4.0 / mean


def occ_wide(occ, half):
    return jnp.concatenate([occ[...]] * (half // LANES), axis=1)


def wide(value, width):
    return jnp.concatenate([value] * (width // LANES), axis=1)


def factor_kernel(chunk, kin, scale, factor):
    bands, plane = factor.shape
    groups = bands // ROWS

    def body(step, carry):
        span = pl.ds(pl.multiple_of(step * chunk, LANES), chunk)
        kinetic = kin[:, span]
        for row in range(0, bands, ROWS):
            y = kinetic * wide(scale[row : row + ROWS, :], chunk)
            square = y * y
            top = (square + 9.0) * (y + 3.0)
            factor[row : row + ROWS, span] = top / (top + square * square)
        return carry

    lax.fori_loop(0, plane // chunk, body, 0)


def weight_kernel(count, bands_all, *refs):
    density, came = refs[0], refs[1 : 1 + count]
    masked, live, base, _, out, onsite_buf = refs[1 + count :]
    bands, half = masked.shape
    total = density[...]
    for ref in came:
        total = total + ref[...]
    onsite = base[...] + (hubbard_weight / bands_all) * total
    atom = lax.broadcasted_iota(jnp.int32, (PMAX, half), 1) // PMAX
    for index in range(half // PMAX):
        onsite_buf[index * PMAX : (index + 1) * PMAX, :] = jnp.where(atom == index, onsite, 0.0)
    kept = masked[...]
    weighted = (
        jnp.dot(kept, onsite_buf[...], precision=HIGH, preferred_element_type=F32) * live[0:1, :]
    )
    rounded = weighted.astype(BF16)
    out[:, 0:half] = rounded
    energy = jnp.sum(kept * rounded.astype(F32), axis=1, keepdims=True)
    energy = jnp.broadcast_to(energy, (bands, LANES))
    head = energy.astype(BF16).astype(F32)
    lane = lax.broadcasted_iota(jnp.int32, (bands, LANES), 1)
    packed = jnp.where(lane == 0, head, jnp.where(lane == 1, energy - head, 0.0))
    out[:, half : half + LANES] = packed.astype(BF16)


def gather_weights(core, mine, theirs, band_kin, norm_inv, weight, shift):
    half = mine.shape[1] - LANES
    weight[:, pl.ds(pl.multiple_of(core * half, LANES), half)] = (
        mine[:, 0:half] * jnp.asarray(step_length, BF16)
    )
    weight[:, pl.ds(pl.multiple_of((1 - core) * half, LANES), half)] = (
        theirs[:, 0:half] * jnp.asarray(step_length, BF16)
    )
    parts = mine[:, half : half + LANES].astype(F32) + theirs[:, half : half + LANES].astype(F32)
    energy = jnp.sum(parts, axis=1, keepdims=True)
    shift[...] = step_length * (band_kin[...] + energy * norm_inv[...])


def moved(current, kin, factor, shift, near, span, chunk, row):
    values = current[row : row + ROWS, span].astype(F32)
    slope = kin[:, span] - wide(shift[row : row + ROWS, :], chunk)
    return values - factor[row : row + ROWS, span] * (slope * values + near[row : row + ROWS, :])


def middle_kernel(
    chunk, core_ref, mine, theirs, band_kin, norm_inv, current, proj, kin, factor, weigh,
    following, own, other, weight, shift, acc, stat_acc,
    near_a, near_b, fresh_a, fresh_b, square_a, square_b,
):
    core = core_ref[0]
    bands, plane = current.shape
    steps = plane // chunk
    nears, freshes, squares = (near_a, near_b), (fresh_a, fresh_b), (square_a, square_b)
    gather_weights(core, mine, theirs, band_kin, norm_inv, weight, shift)

    def span_of(step):
        return pl.ds(pl.multiple_of(step * chunk, LANES), chunk)

    def ahead(step, slot):
        nears[slot][...] = jnp.dot(
            weight[...], proj[:, span_of(step)], preferred_element_type=F32
        )

    def update(step, slot):
        span = span_of(step)
        for row in range(0, bands, ROWS):
            fresh = moved(current, kin, factor, shift, nears[slot], span, chunk, row).astype(BF16)
            following[row : row + ROWS, span] = fresh
            freshes[slot][row : row + ROWS, :] = fresh
            squares[slot][row : row + ROWS, :] = fresh * fresh

    def gather(step, slot):
        span = span_of(step)
        acc[...] += lax.dot_general(
            freshes[slot][...], proj[:, span], NT, preferred_element_type=F32
        )
        stat_acc[...] += lax.dot_general(
            weigh[:, span], squares[slot][...], NT, preferred_element_type=F32
        )

    acc[...] = jnp.zeros_like(acc)
    stat_acc[...] = jnp.zeros_like(stat_acc)
    ahead(0, 0)
    ahead(1, 1)
    update(0, 0)

    def body(pair, carry):
        for offset in (1, 2):
            step, slot = 2 * pair + offset, offset % 2
            ahead(step + 1, 1 - slot)
            gather(step - 1, 1 - slot)
            update(step, slot)
        return carry

    lax.fori_loop(0, steps // 2 - 1, body, 0)
    gather(steps - 2, 0)
    update(steps - 1, 1)
    gather(steps - 1, 1)
    pack_partials(core, acc, stat_acc, own, other)


def last_kernel(
    chunk, core_ref, mine, theirs, band_kin, norm_inv, current, proj, kin, factor,
    out, weight, shift, near_a, near_b, buf_a, buf_b, sems,
):
    core = core_ref[0]
    bands, plane = current.shape
    steps = plane // chunk
    nears, bufs = (near_a, near_b), (buf_a, buf_b)
    gather_weights(core, mine, theirs, band_kin, norm_inv, weight, shift)

    def span_of(step):
        return pl.ds(pl.multiple_of(step * chunk, LANES), chunk)

    def send(step, slot):
        return pltpu.make_async_copy(bufs[slot], out.at[:, span_of(step)], sems.at[slot])

    def ahead(step, slot):
        nears[slot][...] = jnp.dot(
            weight[...], proj[:, span_of(step)], preferred_element_type=F32
        )

    def update(step, slot):
        span = span_of(step)
        for row in range(0, bands, ROWS):
            bufs[slot][row : row + ROWS, :] = moved(
                current, kin, factor, shift, nears[slot], span, chunk, row
            )
        send(step, slot).start()

    ahead(0, 0)
    ahead(1, 1)
    update(0, 0)

    def body(pair, carry):
        for offset in (1, 2):
            step, slot = 2 * pair + offset, offset % 2

            @pl.when(step >= 2)
            def _():
                send(step - 2, slot).wait()

            ahead(step + 1, 1 - slot)
            update(step, slot)
        return carry

    lax.fori_loop(0, steps // 2 - 1, body, 0)
    send(steps - 3, 1).wait()
    update(steps - 1, 1)
    send(steps - 2, 0).wait()
    send(steps - 1, 1).wait()


VM = pl.BlockSpec(memory_space=pltpu.VMEM)
SM = pl.BlockSpec(memory_space=pltpu.SMEM)
HB = pl.BlockSpec(memory_space=pltpu.HBM)


def params(mib):
    return pltpu.CompilerParams(vmem_limit_bytes=mib * MIB)


def swap(value, axis, mask):
    count = lax.axis_size(axis)
    return lax.ppermute(value, axis, [(i, i ^ mask) for i in range(count)])


def masks_direct(count, first):
    return [mask for mask in (first, 2 * first, 3 * first) if mask < count]


def local(
    wave_coeffs, projectors, miller_index, occupations, species_map, proj_counts, onsite_base
):
    bands, plane = wave_coeffs.shape
    slots = projectors.shape[0]
    half = slots // 2
    bands_all = bands * lax.axis_size("gy")
    core = (lax.axis_index("gx") % 2).astype(jnp.int32).reshape(1)
    rows = bands + ROWS * stat_slots(bands, half)
    chunk = min(1024, plane // 4)
    partial_scratch = [pltpu.VMEM((bands, slots), F32), pltpu.VMEM((ROWS, bands), F32)]

    def partial_out(kind):
        return (pltpu.VMEM((rows, half), F32), pltpu.VMEM((rows, half), kind))

    stay = functools.partial(pltpu.with_memory_space_constraint, memory_space=pltpu.HBM)
    current, proj, kin, weigh, live, base, occ, own, other = pl.pallas_call(
        functools.partial(first_kernel, chunk),
        out_shape=(
            pltpu.VMEM(wave_coeffs.shape, BF16),
            pltpu.VMEM(projectors.shape, BF16),
            pltpu.VMEM((ROWS, plane), F32),
            pltpu.VMEM((ROWS, plane), BF16),
            pltpu.VMEM((PMAX, half), F32),
            pltpu.VMEM((PMAX, half), F32),
            pltpu.VMEM((bands, LANES), F32),
        )
        + partial_out(F32),
        in_specs=[SM] + [HB] * 7,
        out_specs=[VM] * 9,
        scratch_shapes=partial_scratch
        + [
            pltpu.VMEM((bands, chunk), BF16),
            pltpu.VMEM(miller_index.shape, jnp.int32),
            pltpu.VMEM((1, bands), F32),
            pltpu.VMEM(onsite_base.shape, F32),
            pltpu.SMEM(species_map.shape, jnp.int32),
            pltpu.SMEM(proj_counts.shape, jnp.int32),
            pltpu.SemaphoreType.DMA((2, plane // chunk)),
            pltpu.SemaphoreType.DMA((5,)),
        ],
        compiler_params=params(12),
    )(
        core, stay(wave_coeffs), stay(projectors), stay(miller_index),
        stay(occupations.reshape(1, bands)), stay(onsite_base), stay(species_map),
        stay(proj_counts),
    )
    for turn in range(ITERS):
        came = swap(other, "gx", 1)
        first = 2
        while True:
            total, sent = pl.pallas_call(
                pair_kernel,
                out_shape=partial_out(F32 if turn + 1 < ITERS else BF16),
                in_specs=[VM, VM],
                out_specs=[VM, VM],
                compiler_params=params(4),
            )(own, came)
            arrived = [swap(sent, "gx", m) for m in masks_direct(lax.axis_size("gx"), first)]
            first *= 4
            if first >= lax.axis_size("gx"):
                break
            own = total
            came = sum(part.astype(F32) for part in arrived)
        masked, density, scale, band_kin, norm_inv = pl.pallas_call(
            functools.partial(density_kernel, len(arrived)),
            out_shape=(
                pltpu.VMEM((bands, half), F32),
                pltpu.VMEM((PMAX, half), F32),
                pltpu.VMEM((bands, LANES), F32),
                pltpu.VMEM((bands, LANES), F32),
                pltpu.VMEM((bands, LANES), F32),
            ),
            in_specs=[VM] * (3 + len(arrived)),
            out_specs=[VM] * 5,
            scratch_shapes=[pltpu.VMEM((ROWS, bands), F32)],
            compiler_params=params(10),
        )(total, *arrived, live, occ)
        others = [swap(density, "gy", m) for m in masks_direct(lax.axis_size("gy"), 1)]
        first = 4
        while first < lax.axis_size("gy"):
            density = density + sum(others)
            others = [swap(density, "gy", m) for m in masks_direct(lax.axis_size("gy"), first)]
            first *= 4
        factor = pl.pallas_call(
            functools.partial(factor_kernel, chunk),
            out_shape=pltpu.VMEM(wave_coeffs.shape, F32),
            in_specs=[VM, VM],
            out_specs=VM,
            compiler_params=params(4),
            cost_estimate=pl.CostEstimate(
                flops=12 * bands * plane, bytes_accessed=4 * bands * plane, transcendentals=0
            ),
        )(kin, scale)
        mine = pl.pallas_call(
            functools.partial(weight_kernel, len(others), bands_all),
            out_shape=pltpu.VMEM((bands, half + LANES), BF16),
            in_specs=[VM] * (5 + len(others)),
            out_specs=VM,
            scratch_shapes=[pltpu.VMEM((half, half), F32)],
            compiler_params=params(6),
        )(density, *others, masked, live, base, factor)
        theirs = swap(mine, "gx", 1)
        held = (core, mine, theirs, band_kin, norm_inv, current, proj, kin, factor)
        gathered = [
            pltpu.VMEM((bands, slots), BF16),
            pltpu.VMEM((bands, LANES), F32),
        ]
        pair = [pltpu.VMEM((bands, chunk), F32)] * 2
        if turn + 1 < ITERS:
            current, own, other = pl.pallas_call(
                functools.partial(middle_kernel, chunk),
                out_shape=(pltpu.VMEM(wave_coeffs.shape, BF16),)
                + partial_out(F32 if turn + 2 < ITERS else BF16),
                in_specs=[SM] + [VM] * 9,
                out_specs=[VM] * 3,
                scratch_shapes=gathered
                + partial_scratch
                + pair
                + [pltpu.VMEM((bands, chunk), BF16)] * 4,
                compiler_params=params(10),
            )(*held, weigh)
    return pl.pallas_call(
        functools.partial(last_kernel, chunk),
        out_shape=jax.ShapeDtypeStruct(wave_coeffs.shape, F32),
        in_specs=[SM] + [VM] * 8,
        out_specs=HB,
        scratch_shapes=gathered + pair + pair + [pltpu.SemaphoreType.DMA((2,))],
        compiler_params=params(10),
    )(*held)


def solution(mesh):
    placed = (P("gy", "gx"), P(None, "gx"), P(None, "gx"), P("gy"), P(), P(), P())
    return jax.shard_map(
        local, mesh=mesh, in_specs=placed, out_specs=P("gy", "gx"), check_vma=False
    )
```

```python
import functools

import jax
import jax.numpy as jnp
from jax import lax
from jax.experimental import pallas as pl
from jax.experimental.pallas import tpu as pltpu
from jax.sharding import PartitionSpec as P

PMAX = 8
ITERS = 2
LANES = 128
MIB = 1 << 20
WIDE = 2
DEEP = 16
FLIGHT_BYTES = 6 * MIB
BUFFERS = 3
CHUNK_FIRST = 2048
CHUNK_MIDDLE = 4096
CHUNK_LAST = 2048
ROWS = 16
F32 = jnp.float32
BF16 = jnp.bfloat16
HIGH = lax.Precision.HIGHEST


kinetic_unit = 1.0 / 600.0
hubbard_weight = 2.0
step_length = 0.5

NT = (((1,), (1,)), ((), ()))
TN = (((0,), (0,)), ((), ()))


def stat_slots(bands, half):
    return -(-bands // half)


def column_of(rows, first, last):
    pick = lax.broadcasted_iota(jnp.int32, (ROWS, LANES), 0)
    ones = jnp.where((pick >= first) & (pick < last), 1.0, 0.0).astype(F32)
    return lax.dot_general(rows, ones, TN, precision=HIGH, preferred_element_type=F32)


def whole_rows(stats):
    row = lax.broadcasted_iota(jnp.int32, stats.shape, 0)
    return jnp.where(row % 2 == 0, stats + pltpu.roll(stats, ROWS - 1, 0), 0.0)


def split_rows(stats):
    head = stats.astype(BF16).astype(F32)
    rest = pltpu.roll(stats - head, 1, 0)
    row = lax.broadcasted_iota(jnp.int32, stats.shape, 0)
    return jnp.where(row % 2 == 0, head, rest).astype(BF16)


def rows_for(stats, kind):
    return split_rows(stats) if kind == BF16 else stats


def pack_partials(core, acc, stats, own, other):
    bands = acc.shape[0]
    half = own.shape[1]
    kind = other.dtype
    own[0:bands, :] = acc[:, pl.ds(pl.multiple_of(core * half, LANES), half)]
    other[0:bands, :] = acc[:, pl.ds(pl.multiple_of((1 - core) * half, LANES), half)].astype(kind)
    row = lax.broadcasted_iota(jnp.int32, stats.shape, 0)
    stats = whole_rows(jnp.where(row < 2, stats, 2.0 * stats))
    split = rows_for(stats, kind)
    for slot in range(stat_slots(bands, half)):
        at = bands + ROWS * slot
        width = min(half, bands - slot * half)
        own[at : at + ROWS, :] = jnp.zeros((ROWS, half), F32)
        other[at : at + ROWS, :] = jnp.zeros((ROWS, half), kind)
        own[at : at + ROWS, 0:width] = stats[:, slot * half : slot * half + width]
        other[at : at + ROWS, 0:width] = split[:, slot * half : slot * half + width]


def stat_rows(norm_acc, kin_acc):
    row = lax.broadcasted_iota(jnp.int32, (ROWS, LANES), 0)
    return lax.dot_general(
        jnp.where(row == 0, 1.0, 0.0).astype(F32), norm_acc[...], NT, precision=HIGH,
        preferred_element_type=F32,
    ) + lax.dot_general(
        jnp.where(row == 2, 1.0, 0.0).astype(F32), kin_acc[...], NT, precision=HIGH,
        preferred_element_type=F32,
    )


def tiles(ref, first, count):
    return jnp.concatenate([ref[first + index] for index in range(count)], axis=1)


def first_kernel(
    chunk, flight, core_ref, wave, proj, miller, occ, base, species_hbm, counts_hbm,
    bands_out, proj_out, kin_out, live_out, base_out, occ_out, own, other,
    wave_buf, proj_buf, acc, norm_acc, kin_acc, miller_buf, occ_buf, base_buf, species, counts, sems, small_sems,
):
    core = core_ref[0]
    bands, plane = wave.shape
    steps = plane // chunk
    count = chunk // LANES
    half = own.shape[1]
    small = [
        pltpu.make_async_copy(source, target, small_sems.at[index])
        for index, (source, target) in enumerate(
            (
                (miller, miller_buf),
                (occ, occ_buf),
                (base, base_buf),
                (species_hbm, species),
                (counts_hbm, counts),
            )
        )
    ]
    for copy in small:
        copy.start()

    def copies(step):
        span = pl.ds(step * chunk, chunk)
        slot = lax.rem(step, flight)
        return (
            pltpu.make_async_copy(wave.at[:, span], wave_buf.at[slot], sems.at[0, slot]),
            pltpu.make_async_copy(proj.at[:, span], proj_buf.at[slot], sems.at[1, slot]),
        )

    for step in range(min(flight, steps)):
        for copy in copies(step):
            copy.start()
    acc[...] = jnp.zeros_like(acc)
    norm_acc[...] = jnp.zeros_like(norm_acc)
    kin_acc[...] = jnp.zeros_like(kin_acc)
    for copy in small:
        copy.wait()

    lane = lax.broadcasted_iota(jnp.int32, (PMAX, half), 1)
    slot = lane % PMAX
    atom = lane // PMAX
    atoms_half = half // PMAX

    def tables(index, held):
        count_row, kind_row = held
        here = atom == index
        source = core * atoms_half + index
        return (
            jnp.where(here, counts[source], count_row),
            jnp.where(here, species[source], kind_row),
        )

    zero = jnp.zeros((PMAX, half), jnp.int32)
    count_row, kind_row = lax.fori_loop(0, atoms_half, tables, (zero, zero))
    live_out[...] = jnp.where(slot < count_row, 1.0, 0.0).astype(F32)
    spread = jnp.where(
        lane == lane // PMAX * PMAX + lax.broadcasted_iota(jnp.int32, (PMAX, half), 0), 1.0, 0.0
    ).astype(F32)
    table = jnp.zeros((PMAX, half), F32)
    for kind in range(base.shape[0]):
        block = base_buf[kind]
        symmetric = 0.5 * (
            lax.dot_general(
                block, spread, (((1,), (0,)), ((), ())), precision=HIGH, preferred_element_type=F32
            )
            + lax.dot_general(block, spread, TN, precision=HIGH, preferred_element_type=F32)
        )
        table = jnp.where(kind_row == kind, symmetric, table)
    base_out[...] = table
    occ_rows = jnp.broadcast_to(occ_buf[...], (ROWS, bands))
    occ_out[...] = column_of(occ_rows, 0, 1)

    def step_body(step, carry):
        span = pl.ds(pl.multiple_of(step * chunk, LANES), chunk)
        parts = miller_buf[:, span].astype(F32)
        m0, m1, m2 = parts[0:1], parts[1:2], parts[2:3]
        kinetic = (1.5 * m0 * m0 + m1 * m1 + 0.5 * m2 * m2) * kinetic_unit
        halved = jnp.broadcast_to(step_length * kinetic, (PMAX, chunk))
        kin_out[:, span] = halved
        for copy in copies(step):
            copy.wait()
        slot = lax.rem(step, flight)
        values = wave_buf[slot]
        others = proj_buf[slot]
        for index in range(count):
            lanes = slice(index * LANES, (index + 1) * LANES)
            bands_out[step * count + index] = values[:, lanes]
            proj_out[step * count + index] = others[:, lanes]
        acc[...] += lax.dot_general(values, others, NT, preferred_element_type=F32)
        for row in range(0, bands, ROWS):
            norm = kin_sum = jnp.zeros((ROWS, LANES), F32)
            for index in range(count):
                lanes = slice(index * LANES, (index + 1) * LANES)
                square = values[row : row + ROWS, lanes].astype(F32)
                square = square * square
                norm = norm + square
                kin_sum = kin_sum + square * jnp.concatenate([halved[:, lanes]] * 2, axis=0)
            norm_acc[row : row + ROWS, :] += norm
            kin_acc[row : row + ROWS, :] += kin_sum

        @pl.when(step + flight < steps)
        def _():
            for copy in copies(step + flight):
                copy.start()

        return carry

    lax.fori_loop(0, steps, step_body, 0)
    pack_partials(core, acc, stat_rows(norm_acc, kin_acc), own, other)


def pair_kernel(own, came, total, sent):
    rows, half = own.shape
    kind = sent.dtype
    value = own[...] + came[...].astype(F32)
    total[...] = value
    sent[...] = value.astype(kind)
    bands = rows - ROWS * stat_slots_of(rows, half)
    if kind == BF16:
        for at in range(bands, rows, ROWS):
            whole = whole_rows(value[at : at + ROWS])
            total[at : at + ROWS, :] = whole
            sent[at : at + ROWS, :] = split_rows(whole)


def stat_slots_of(rows, half):
    slots = 1
    while stat_slots(rows - ROWS * slots, half) != slots:
        slots += 1
    return slots


def density_kernel(count, *refs):
    total, came = refs[0], refs[1 : 1 + count]
    live, occ, masked, density, scale, band_kin, norm_inv, rows_buf = refs[1 + count :]
    rows, half = total.shape
    bands = masked.shape[0]
    value = total[...]
    for ref in came:
        value = value + ref[...].astype(F32)
    kept = value[0:bands] * live[0:1, :]
    masked[...] = kept
    full = lax.dot_general(
        kept * occ_wide(occ, half), kept, TN, precision=HIGH, preferred_element_type=F32
    )
    atom = lax.broadcasted_iota(jnp.int32, (PMAX, half), 1) // PMAX
    compact = jnp.zeros((PMAX, half), F32)
    for index in range(half // PMAX):
        block = full[index * PMAX : (index + 1) * PMAX]
        compact = jnp.where(atom == index, block, compact)
    density[...] = compact
    for slot in range(stat_slots(bands, half)):
        at = bands + ROWS * slot
        width = min(half, bands - slot * half)
        rows_buf[:, slot * half : slot * half + width] = value[at : at + ROWS, 0:width]
    norm = column_of(rows_buf[...], 0, 2)
    kin = column_of(rows_buf[...], 2, 4)
    mean = kin / norm
    band_kin[...] = mean
    norm_inv[...] = 1.0 / norm
    scale[...] = 4.0 / mean


def occ_wide(occ, half):
    return jnp.concatenate([occ[...]] * (half // LANES), axis=1)


def wide(value, width):
    return jnp.concatenate([value] * (width // LANES), axis=1)


def factor_kernel(chunk, kin, scale, factor):
    bands, plane = factor.shape

    def body(step, carry):
        span = pl.ds(pl.multiple_of(step * chunk, LANES), chunk)
        kinetic = kin[:, span]
        for row in range(0, bands, PMAX):
            y = kinetic * wide(scale[row : row + PMAX, :], chunk)
            square = y * y
            top = (square + 9.0) * (y + 3.0)
            factor[row : row + PMAX, span] = top / (top + square * square)
        return carry

    lax.fori_loop(0, plane // chunk, body, 0)


def weight_kernel(count, bands_all, *refs):
    density, came = refs[0], refs[1 : 1 + count]
    masked, live, base, _, out, onsite_buf = refs[1 + count :]
    bands, half = masked.shape
    total = density[...]
    for ref in came:
        total = total + ref[...]
    onsite = base[...] + (hubbard_weight / bands_all) * total
    atom = lax.broadcasted_iota(jnp.int32, (PMAX, half), 1) // PMAX
    for index in range(half // PMAX):
        onsite_buf[index * PMAX : (index + 1) * PMAX, :] = jnp.where(atom == index, onsite, 0.0)
    kept = masked[...]
    weighted = (
        jnp.dot(kept, onsite_buf[...], precision=HIGH, preferred_element_type=F32) * live[0:1, :]
    )
    rounded = weighted.astype(BF16)
    out[:, 0:half] = rounded
    energy = jnp.sum(kept * rounded.astype(F32), axis=1, keepdims=True)
    energy = jnp.broadcast_to(energy, (bands, LANES))
    head = energy.astype(BF16).astype(F32)
    lane = lax.broadcasted_iota(jnp.int32, (bands, LANES), 1)
    packed = jnp.where(lane == 0, head, jnp.where(lane == 1, energy - head, 0.0))
    out[:, half : half + LANES] = packed.astype(BF16)


def gather_weights(core, mine, theirs, band_kin, norm_inv, weight, shift):
    half = mine.shape[1] - LANES
    weight[:, pl.ds(pl.multiple_of(core * half, LANES), half)] = (
        mine[:, 0:half] * jnp.asarray(step_length, BF16)
    )
    weight[:, pl.ds(pl.multiple_of((1 - core) * half, LANES), half)] = (
        theirs[:, 0:half] * jnp.asarray(step_length, BF16)
    )
    parts = mine[:, half : half + LANES].astype(F32) + theirs[:, half : half + LANES].astype(F32)
    energy = jnp.sum(parts, axis=1, keepdims=True)
    shift[...] = step_length * (band_kin[...] + energy * norm_inv[...])


def moved(current, kinetic, factor, shift, near, step, count, row, index):
    rows = slice(row, row + ROWS)
    tile = step * count + index
    span = pl.ds(pl.multiple_of(tile * LANES, LANES), LANES)
    values = current[tile, rows, :].astype(F32)
    slope = kinetic - shift[rows, :]
    near_here = near[rows, index * LANES : (index + 1) * LANES]
    return values - factor[rows, span] * (slope * values + near_here)


def kinetic_tile(kin, tile):
    row = kin[:, pl.ds(pl.multiple_of(tile * LANES, LANES), LANES)]
    return jnp.concatenate([row] * (ROWS // PMAX), axis=0)


def middle_kernel(
    chunk, core_ref, mine, theirs, band_kin, norm_inv, current, proj, kin, factor,
    following, own, other, weight, shift, acc, norm_acc, kin_acc,
    near_a, near_b, fresh_a, fresh_b,
):
    core = core_ref[0]
    bands = current.shape[1]
    count = chunk // LANES
    steps = current.shape[0] // count
    nears, freshes = (near_a, near_b), (fresh_a, fresh_b)
    gather_weights(core, mine, theirs, band_kin, norm_inv, weight, shift)

    def ahead(step, slot, index):
        nears[slot][:, index * LANES : (index + WIDE) * LANES] = jnp.dot(
            weight[...], tiles(proj, step * count + index, WIDE), preferred_element_type=F32
        )

    def update(step, slot, first):
        for row in range(0, bands, ROWS):
            norm = kin_sum = jnp.zeros((ROWS, LANES), F32)
            for index in range(first, first + WIDE):
                kinetic = kinetic_tile(kin, step * count + index)
                value = moved(
                    current, kinetic, factor, shift, nears[slot], step, count, row, index
                )
                fresh = value.astype(BF16)
                following[step * count + index, row : row + ROWS, :] = fresh
                freshes[slot][index, row : row + ROWS, :] = fresh
                square = value * value
                norm = norm + square
                kin_sum = kin_sum + square * kinetic
            norm_acc[row : row + ROWS, :] += norm
            kin_acc[row : row + ROWS, :] += kin_sum

    def gather(step, slot, index):
        acc[...] += lax.dot_general(
            tiles(freshes[slot], index, DEEP), tiles(proj, step * count + index, DEEP), NT,
            preferred_element_type=F32,
        )

    parts = range(0, count, WIDE)

    acc[...] = jnp.zeros_like(acc)
    norm_acc[...] = jnp.zeros_like(norm_acc)
    kin_acc[...] = jnp.zeros_like(kin_acc)
    for index in parts:
        ahead(0, 0, index)
    for index in parts:
        ahead(1, 1, index)
        update(0, 0, index)

    def body(pair, carry):
        for offset in (1, 2):
            step, slot = 2 * pair + offset, offset % 2
            for index in parts:
                ahead(step + 1, 1 - slot, index)
                if index % DEEP == 0:
                    gather(step - 1, 1 - slot, index)
                update(step, slot, index)
        return carry

    lax.fori_loop(0, steps // 2 - 1, body, 0)
    for index in parts:
        if index % DEEP == 0:
            gather(steps - 2, 0, index)
        update(steps - 1, 1, index)
    for index in range(0, count, DEEP):
        gather(steps - 1, 1, index)
    pack_partials(core, acc, stat_rows(norm_acc, kin_acc), own, other)


def last_kernel(
    chunk, core_ref, mine, theirs, band_kin, norm_inv, current, proj, kin, factor,
    out, weight, shift, near_a, near_b, bufs, sems,
):
    core = core_ref[0]
    bands = current.shape[1]
    count = chunk // LANES
    steps = current.shape[0] // count
    nears = (near_a, near_b)
    gather_weights(core, mine, theirs, band_kin, norm_inv, weight, shift)

    def send(step):
        slot = lax.rem(step, BUFFERS)
        span = pl.ds(pl.multiple_of(step * chunk, LANES), chunk)
        return pltpu.make_async_copy(bufs.at[slot], out.at[:, span], sems.at[slot])

    def ahead(step, side, index):
        nears[side][:, index * LANES : (index + WIDE) * LANES] = jnp.dot(
            weight[...], tiles(proj, step * count + index, WIDE), preferred_element_type=F32
        )

    def update(step, side, first):
        slot = lax.rem(step, BUFFERS)
        for row in range(0, bands, ROWS):
            for index in range(first, first + WIDE):
                kinetic = kinetic_tile(kin, step * count + index)
                bufs[slot, row : row + ROWS, index * LANES : (index + 1) * LANES] = moved(
                    current, kinetic, factor, shift, nears[side], step, count, row, index
                )

    parts = range(0, count, WIDE)
    for index in parts:
        ahead(0, 0, index)

    def body(pair, carry):
        for side in range(2):
            step = 2 * pair + side

            @pl.when(step >= BUFFERS)
            def _():
                send(step - BUFFERS).wait()

            for index in parts:
                ahead(jnp.minimum(step + 1, steps - 1), 1 - side, index)
                update(step, side, index)
            send(step).start()
        return carry

    lax.fori_loop(0, steps // 2, body, 0)
    for step in range(max(0, steps - BUFFERS), steps):
        send(step).wait()


VM = pl.BlockSpec(memory_space=pltpu.VMEM)
SM = pl.BlockSpec(memory_space=pltpu.SMEM)
HB = pl.BlockSpec(memory_space=pltpu.HBM)


def params(mib):
    return pltpu.CompilerParams(vmem_limit_bytes=mib * MIB)


def swap(value, axis, mask):
    count = lax.axis_size(axis)
    return lax.ppermute(value, axis, [(i, i ^ mask) for i in range(count)])


def masks_direct(count, first):
    return [mask for mask in (first, 2 * first, 3 * first) if mask < count]


def local(
    wave_coeffs, projectors, miller_index, occupations, species_map, proj_counts, onsite_base
):
    bands, plane = wave_coeffs.shape
    slots = projectors.shape[0]
    half = slots // 2
    bands_all = bands * lax.axis_size("gy")
    core = (lax.axis_index("gx") % 2).astype(jnp.int32).reshape(1)
    rows = bands + ROWS * stat_slots(bands, half)
    chunk_first = min(CHUNK_FIRST, plane // 2)
    chunk_middle = min(CHUNK_MIDDLE, plane // 4)
    chunk_last = min(CHUNK_LAST, plane // 4)
    chunk_factor = min(1024, plane)
    def partial_out(kind):
        return (pltpu.VMEM((rows, half), F32), pltpu.VMEM((rows, half), kind))

    stay = functools.partial(pltpu.with_memory_space_constraint, memory_space=pltpu.HBM)
    count = plane // LANES
    flight = max(2, FLIGHT_BYTES // (2 * (bands + slots) * chunk_first))
    band_tiles = pltpu.VMEM((count, bands, LANES), BF16)
    current, proj, kin, live, base, occ, own, other = pl.pallas_call(
        functools.partial(first_kernel, chunk_first, flight),
        out_shape=(
            band_tiles,
            pltpu.VMEM((count, slots, LANES), BF16),
            pltpu.VMEM((PMAX, plane), F32),
            pltpu.VMEM((PMAX, half), F32),
            pltpu.VMEM((PMAX, half), F32),
            pltpu.VMEM((bands, LANES), F32),
        )
        + partial_out(F32),
        in_specs=[SM] + [HB] * 7,
        out_specs=[VM] * 8,
        scratch_shapes=[
            pltpu.VMEM((flight, bands, chunk_first), BF16),
            pltpu.VMEM((flight, slots, chunk_first), BF16),
        ]
        + [pltpu.VMEM((bands, slots), F32)]
        + [pltpu.VMEM((bands, LANES), F32)] * 2
        + [
            pltpu.VMEM(miller_index.shape, jnp.int32),
            pltpu.VMEM((1, bands), F32),
            pltpu.VMEM(onsite_base.shape, F32),
            pltpu.SMEM(species_map.shape, jnp.int32),
            pltpu.SMEM(proj_counts.shape, jnp.int32),
            pltpu.SemaphoreType.DMA((2, flight)),
            pltpu.SemaphoreType.DMA((5,)),
        ],
        compiler_params=params(12),
    )(
        core, stay(wave_coeffs), stay(projectors), stay(miller_index),
        stay(occupations.reshape(1, bands)), stay(onsite_base), stay(species_map),
        stay(proj_counts),
    )
    for turn in range(ITERS):
        came = swap(other, "gx", 1)
        first = 2
        while True:
            total, sent = pl.pallas_call(
                pair_kernel,
                out_shape=partial_out(F32 if turn + 1 < ITERS else BF16),
                in_specs=[VM, VM],
                out_specs=[VM, VM],
                compiler_params=params(4),
            )(own, came)
            arrived = [swap(sent, "gx", m) for m in masks_direct(lax.axis_size("gx"), first)]
            first *= 4
            if first >= lax.axis_size("gx"):
                break
            own = total
            came = sum(part.astype(F32) for part in arrived)
        masked, density, scale, band_kin, norm_inv = pl.pallas_call(
            functools.partial(density_kernel, len(arrived)),
            out_shape=(
                pltpu.VMEM((bands, half), F32),
                pltpu.VMEM((PMAX, half), F32),
                pltpu.VMEM((bands, LANES), F32),
                pltpu.VMEM((bands, LANES), F32),
                pltpu.VMEM((bands, LANES), F32),
            ),
            in_specs=[VM] * (3 + len(arrived)),
            out_specs=[VM] * 5,
            scratch_shapes=[pltpu.VMEM((ROWS, bands), F32)],
            compiler_params=params(10),
        )(total, *arrived, live, occ)
        others = [swap(density, "gy", m) for m in masks_direct(lax.axis_size("gy"), 1)]
        first = 4
        while first < lax.axis_size("gy"):
            density = density + sum(others)
            others = [swap(density, "gy", m) for m in masks_direct(lax.axis_size("gy"), first)]
            first *= 4
        factor = pl.pallas_call(
            functools.partial(factor_kernel, chunk_factor),
            out_shape=pltpu.VMEM(wave_coeffs.shape, F32),
            in_specs=[VM, VM],
            out_specs=VM,
            compiler_params=params(4),
            cost_estimate=pl.CostEstimate(
                flops=12 * bands * plane, bytes_accessed=4 * bands * plane, transcendentals=0
            ),
        )(kin, scale)
        mine = pl.pallas_call(
            functools.partial(weight_kernel, len(others), bands_all),
            out_shape=pltpu.VMEM((bands, half + LANES), BF16),
            in_specs=[VM] * (5 + len(others)),
            out_specs=VM,
            scratch_shapes=[pltpu.VMEM((half, half), F32)],
            compiler_params=params(6),
        )(density, *others, masked, live, base, factor)
        theirs = swap(mine, "gx", 1)
        held = (core, mine, theirs, band_kin, norm_inv, current, proj, kin, factor)
        gathered = [
            pltpu.VMEM((bands, slots), BF16),
            pltpu.VMEM((bands, LANES), F32),
        ]
        if turn + 1 < ITERS:
            current, own, other = pl.pallas_call(
                functools.partial(middle_kernel, chunk_middle),
                out_shape=(band_tiles,)
                + partial_out(F32 if turn + 2 < ITERS else BF16),
                in_specs=[SM] + [VM] * 8,
                out_specs=[VM] * 3,
                scratch_shapes=gathered
                + [pltpu.VMEM((bands, slots), F32)]
                + [pltpu.VMEM((bands, LANES), F32)] * 2
                + [pltpu.VMEM((bands, chunk_middle), F32)] * 2
                + [pltpu.VMEM((chunk_middle // LANES, bands, LANES), BF16)] * 2,
                compiler_params=params(13),
            )(*held)
    return pl.pallas_call(
        functools.partial(last_kernel, chunk_last),
        out_shape=jax.ShapeDtypeStruct(wave_coeffs.shape, F32),
        in_specs=[SM] + [VM] * 8,
        out_specs=HB,
        scratch_shapes=gathered
        + [pltpu.VMEM((bands, chunk_last), F32)] * 2
        + [pltpu.VMEM((BUFFERS, bands, chunk_last), F32), pltpu.SemaphoreType.DMA((BUFFERS,))],
        compiler_params=params(11),
    )(*held)


def solution(mesh):
    placed = (P("gy", "gx"), P(None, "gx"), P(None, "gx"), P("gy"), P(), P(), P())
    return jax.shard_map(
        local, mesh=mesh, in_specs=placed, out_specs=P("gy", "gx"), check_vma=False
    )
```

```python
import functools

import jax
import jax.numpy as jnp
from jax import lax
from jax.experimental import pallas as pl
from jax.experimental.pallas import tpu as pltpu
from jax.sharding import PartitionSpec as P

PMAX = 8
ITERS = 2
LANES = 128
MIB = 1 << 20
WIDE = 2
DEEP = 16
FLIGHT_BYTES = 6 * MIB
BUFFERS = 3
SPLIT = 4
SHARE = 11
CHUNK_FIRST = 2048
CHUNK_MIDDLE = 4096
CHUNK_LAST = 2048
ROWS = 16
STATS = 4
F32 = jnp.float32
BF16 = jnp.bfloat16
HIGH = lax.Precision.HIGHEST


kinetic_unit = 1.0 / 600.0
hubbard_weight = 2.0
step_length = 0.5

NT = (((1,), (1,)), ((), ()))
TN = (((0,), (0,)), ((), ()))


def stat_slots(bands, half):
    return -(-bands // half)


def column_of(rows, first, last):
    pick = lax.broadcasted_iota(jnp.int32, (ROWS, LANES), 0)
    ones = jnp.where((pick >= first) & (pick < last), 1.0, 0.0).astype(F32)
    return lax.dot_general(rows, ones, TN, precision=HIGH, preferred_element_type=F32)


def whole_rows(stats):
    row = lax.broadcasted_iota(jnp.int32, stats.shape, 0)
    return jnp.where(row % 2 == 0, stats + pltpu.roll(stats, ROWS - 1, 0), 0.0)


def split_rows(stats):
    head = stats.astype(BF16).astype(F32)
    rest = pltpu.roll(stats - head, 1, 0)
    row = lax.broadcasted_iota(jnp.int32, stats.shape, 0)
    return jnp.where(row % 2 == 0, head, rest).astype(BF16)


def rows_for(stats, kind):
    return split_rows(stats) if kind == BF16 else stats


def pack_partials(core, acc, stats, own, other):
    bands = acc.shape[0]
    half = own.shape[1]
    kind = other.dtype
    own[0:bands, :] = acc[:, pl.ds(pl.multiple_of(core * half, LANES), half)]
    other[0:bands, :] = acc[:, pl.ds(pl.multiple_of((1 - core) * half, LANES), half)].astype(kind)
    row = lax.broadcasted_iota(jnp.int32, stats.shape, 0)
    stats = whole_rows(jnp.where(row < 2, stats, 2.0 * stats))
    at = bands
    own[at : at + ROWS, :] = jnp.zeros((ROWS, half), F32)
    for slot in range(stat_slots(bands, half)):
        width = min(half, bands - slot * half)
        lift = slice(STATS * slot, STATS * (slot + 1))
        lifted = pltpu.roll(stats, STATS * slot, 0) if slot else stats
        own[at + lift.start : at + lift.stop, 0:width] = lifted[
            lift, slot * half : slot * half + width
        ]
    other[at : at + ROWS, :] = rows_for(own[at : at + ROWS, :], kind)


def stat_rows(norm_acc, kin_acc):
    row = lax.broadcasted_iota(jnp.int32, (ROWS, LANES), 0)
    return lax.dot_general(
        jnp.where(row == 0, 1.0, 0.0).astype(F32), norm_acc[...], NT, precision=HIGH,
        preferred_element_type=F32,
    ) + lax.dot_general(
        jnp.where(row == 2, 1.0, 0.0).astype(F32), kin_acc[...], NT, precision=HIGH,
        preferred_element_type=F32,
    )


def tiles(ref, first, count):
    return jnp.concatenate([ref[first + index] for index in range(count)], axis=1)


def first_kernel(
    chunk, flight, core_ref, wave, proj, miller, occ, base, species_hbm, counts_hbm,
    bands_out, proj_out, kin_out, live_out, base_out, occ_out, own, other,
    wave_buf, proj_buf, acc, norm_acc, kin_acc, miller_buf, occ_buf, base_buf, species, counts, sems, small_sems,
):
    core = core_ref[0]
    bands, plane = wave.shape
    steps = plane // chunk
    count = chunk // LANES
    half = own.shape[1]
    small = [
        pltpu.make_async_copy(source, target, small_sems.at[index])
        for index, (source, target) in enumerate(
            (
                (miller, miller_buf),
                (occ, occ_buf),
                (base, base_buf),
                (species_hbm, species),
                (counts_hbm, counts),
            )
        )
    ]
    for copy in small:
        copy.start()

    def copies(step):
        span = pl.ds(step * chunk, chunk)
        slot = lax.rem(step, flight)
        return (
            pltpu.make_async_copy(wave.at[:, span], wave_buf.at[slot], sems.at[0, slot]),
            pltpu.make_async_copy(proj.at[:, span], proj_buf.at[slot], sems.at[1, slot]),
        )

    for step in range(min(flight, steps)):
        for copy in copies(step):
            copy.start()
    acc[...] = jnp.zeros_like(acc)
    norm_acc[...] = jnp.zeros_like(norm_acc)
    kin_acc[...] = jnp.zeros_like(kin_acc)
    for copy in small:
        copy.wait()

    lane = lax.broadcasted_iota(jnp.int32, (PMAX, half), 1)
    slot = lane % PMAX
    atom = lane // PMAX
    atoms_half = half // PMAX

    def tables(index, held):
        count_row, kind_row = held
        here = atom == index
        source = core * atoms_half + index
        return (
            jnp.where(here, counts[source], count_row),
            jnp.where(here, species[source], kind_row),
        )

    zero = jnp.zeros((PMAX, half), jnp.int32)
    count_row, kind_row = lax.fori_loop(0, atoms_half, tables, (zero, zero))
    live_out[...] = jnp.where(slot < count_row, 1.0, 0.0).astype(F32)
    spread = jnp.where(
        lane == lane // PMAX * PMAX + lax.broadcasted_iota(jnp.int32, (PMAX, half), 0), 1.0, 0.0
    ).astype(F32)
    table = jnp.zeros((PMAX, half), F32)
    for kind in range(base.shape[0]):
        block = base_buf[kind]
        symmetric = 0.5 * (
            lax.dot_general(
                block, spread, (((1,), (0,)), ((), ())), precision=HIGH, preferred_element_type=F32
            )
            + lax.dot_general(block, spread, TN, precision=HIGH, preferred_element_type=F32)
        )
        table = jnp.where(kind_row == kind, symmetric, table)
    base_out[...] = table
    occ_rows = jnp.broadcast_to(occ_buf[...], (ROWS, bands))
    occ_out[...] = column_of(occ_rows, 0, 1)

    def step_body(step, carry):
        span = pl.ds(pl.multiple_of(step * chunk, LANES), chunk)
        parts = miller_buf[:, span].astype(F32)
        m0, m1, m2 = parts[0:1], parts[1:2], parts[2:3]
        kinetic = (1.5 * m0 * m0 + m1 * m1 + 0.5 * m2 * m2) * kinetic_unit
        halved = jnp.broadcast_to(step_length * kinetic, (PMAX, chunk))
        kin_out[:, span] = halved
        for copy in copies(step):
            copy.wait()
        slot = lax.rem(step, flight)
        values = wave_buf[slot]
        others = proj_buf[slot]
        for index in range(count):
            lanes = slice(index * LANES, (index + 1) * LANES)
            bands_out[step * count + index] = values[:, lanes]
            proj_out[step * count + index] = others[:, lanes]
        acc[...] += lax.dot_general(values, others, NT, preferred_element_type=F32)
        for row in range(0, bands, ROWS):
            norm = kin_sum = jnp.zeros((ROWS, LANES), F32)
            for index in range(count):
                lanes = slice(index * LANES, (index + 1) * LANES)
                square = values[row : row + ROWS, lanes].astype(F32)
                square = square * square
                norm = norm + square
                kin_sum = kin_sum + square * jnp.concatenate([halved[:, lanes]] * 2, axis=0)
            norm_acc[row : row + ROWS, :] += norm
            kin_acc[row : row + ROWS, :] += kin_sum

        @pl.when(step + flight < steps)
        def _():
            for copy in copies(step + flight):
                copy.start()

        return carry

    lax.fori_loop(0, steps, step_body, 0)
    pack_partials(core, acc, stat_rows(norm_acc, kin_acc), own, other)


def pair_kernel(own, came, total, sent):
    rows, half = own.shape
    kind = sent.dtype
    value = own[...] + came[...].astype(F32)
    total[...] = value
    sent[...] = value.astype(kind)
    if kind == BF16:
        whole = whole_rows(value[rows - ROWS :])
        total[rows - ROWS :, :] = whole
        sent[rows - ROWS :, :] = split_rows(whole)


def density_kernel(count, *refs):
    total, came = refs[0], refs[1 : 1 + count]
    live, occ, masked, density, scale, band_kin, norm_inv, rows_buf = refs[1 + count :]
    rows, half = total.shape
    bands = masked.shape[0]
    value = total[...]
    for ref in came:
        value = value + ref[...].astype(F32)
    kept = value[0:bands] * live[0:1, :]
    masked[...] = kept
    full = lax.dot_general(
        kept * occ_wide(occ, half), kept, TN, precision=HIGH, preferred_element_type=F32
    )
    atom = lax.broadcasted_iota(jnp.int32, (PMAX, half), 1) // PMAX
    compact = jnp.zeros((PMAX, half), F32)
    for index in range(half // PMAX):
        block = full[index * PMAX : (index + 1) * PMAX]
        compact = jnp.where(atom == index, block, compact)
    density[...] = compact
    block = value[bands:]
    for slot in range(stat_slots(bands, half)):
        width = min(half, bands - slot * half)
        lowered = pltpu.roll(block, ROWS - STATS * slot, 0) if slot else block
        rows_buf[:, slot * half : slot * half + width] = lowered[:, 0:width]
    norm = column_of(rows_buf[...], 0, 2)
    kin = column_of(rows_buf[...], 2, 4)
    mean = kin / norm
    band_kin[...] = mean
    norm_inv[...] = 1.0 / norm
    scale[...] = 4.0 / mean


def occ_wide(occ, half):
    return jnp.concatenate([occ[...]] * (half // LANES), axis=1)


def wide(value, width):
    return jnp.concatenate([value] * (width // LANES), axis=1)


def fill_factor(chunk, first, last, kin, scale, factor):
    bands = factor.shape[0]

    def body(step, carry):
        span = pl.ds(pl.multiple_of(step * chunk, LANES), chunk)
        kinetic = kin[:, span]
        for row in range(0, bands, PMAX):
            y = kinetic * wide(scale[row : row + PMAX, :], chunk)
            square = y * y
            top = (square + 9.0) * (y + 3.0)
            factor[row : row + PMAX, span] = top / (top + square * square)
        return carry

    lax.fori_loop(first, last, body, 0)


def factor_kernel(chunk, first, last, kin, scale, factor, done):
    fill_factor(chunk, first, last, kin, scale, factor)
    done[...] = scale[0:PMAX, :]


def factor_rest_kernel(chunk, first, last, begun, kin, scale, after, factor):
    fill_factor(chunk, first, last, kin, scale, factor)


def weight_kernel(count, bands_all, *refs):
    density, came = refs[0], refs[1 : 1 + count]
    masked, live, base, _, out, onsite_buf = refs[1 + count :]
    bands, half = masked.shape
    total = density[...]
    for ref in came:
        total = total + ref[...]
    onsite = base[...] + (hubbard_weight / bands_all) * total
    atom = lax.broadcasted_iota(jnp.int32, (PMAX, half), 1) // PMAX
    for index in range(half // PMAX):
        onsite_buf[index * PMAX : (index + 1) * PMAX, :] = jnp.where(atom == index, onsite, 0.0)
    kept = masked[...]
    weighted = (
        jnp.dot(kept, onsite_buf[...], precision=HIGH, preferred_element_type=F32) * live[0:1, :]
    )
    rounded = weighted.astype(BF16)
    out[:, 0:half] = rounded
    energy = jnp.sum(kept * rounded.astype(F32), axis=1, keepdims=True)
    energy = jnp.broadcast_to(energy, (bands, LANES))
    head = energy.astype(BF16).astype(F32)
    lane = lax.broadcasted_iota(jnp.int32, (bands, LANES), 1)
    packed = jnp.where(lane == 0, head, jnp.where(lane == 1, energy - head, 0.0))
    out[:, half : half + LANES] = packed.astype(BF16)


def gather_weights(core, mine, theirs, band_kin, norm_inv, weight, shift):
    half = mine.shape[1] - LANES
    weight[:, pl.ds(pl.multiple_of(core * half, LANES), half)] = (
        mine[:, 0:half] * jnp.asarray(step_length, BF16)
    )
    weight[:, pl.ds(pl.multiple_of((1 - core) * half, LANES), half)] = (
        theirs[:, 0:half] * jnp.asarray(step_length, BF16)
    )
    parts = mine[:, half : half + LANES].astype(F32) + theirs[:, half : half + LANES].astype(F32)
    energy = jnp.sum(parts, axis=1, keepdims=True)
    shift[...] = step_length * (band_kin[...] + energy * norm_inv[...])


def moved(current, kinetic, factor, shift, near, step, count, row, index):
    rows = slice(row, row + ROWS)
    tile = step * count + index
    span = pl.ds(pl.multiple_of(tile * LANES, LANES), LANES)
    values = current[tile, rows, :].astype(F32)
    slope = kinetic - shift[rows, :]
    near_here = near[rows, index * LANES : (index + 1) * LANES]
    return values - factor[rows, span] * (slope * values + near_here)


def kinetic_tile(kin, tile):
    row = kin[:, pl.ds(pl.multiple_of(tile * LANES, LANES), LANES)]
    return jnp.concatenate([row] * (ROWS // PMAX), axis=0)


def middle_kernel(
    chunk, core_ref, mine, theirs, band_kin, norm_inv, current, proj, kin, factor,
    following, own, other, weight, shift, acc, norm_acc, kin_acc,
    near_a, near_b, fresh_a, fresh_b,
):
    core = core_ref[0]
    bands = current.shape[1]
    count = chunk // LANES
    steps = current.shape[0] // count
    nears, freshes = (near_a, near_b), (fresh_a, fresh_b)
    gather_weights(core, mine, theirs, band_kin, norm_inv, weight, shift)

    def ahead(step, slot, index):
        nears[slot][:, index * LANES : (index + WIDE) * LANES] = jnp.dot(
            weight[...], tiles(proj, step * count + index, WIDE), preferred_element_type=F32
        )

    def update(step, slot, first):
        for row in range(0, bands, ROWS):
            norm = kin_sum = jnp.zeros((ROWS, LANES), F32)
            for index in range(first, first + WIDE):
                kinetic = kinetic_tile(kin, step * count + index)
                value = moved(
                    current, kinetic, factor, shift, nears[slot], step, count, row, index
                )
                fresh = value.astype(BF16)
                following[step * count + index, row : row + ROWS, :] = fresh
                freshes[slot][index, row : row + ROWS, :] = fresh
                square = value * value
                norm = norm + square
                kin_sum = kin_sum + square * kinetic
            norm_acc[row : row + ROWS, :] += norm
            kin_acc[row : row + ROWS, :] += kin_sum

    def gather(step, slot, index):
        acc[...] += lax.dot_general(
            tiles(freshes[slot], index, DEEP), tiles(proj, step * count + index, DEEP), NT,
            preferred_element_type=F32,
        )

    parts = range(0, count, WIDE)

    acc[...] = jnp.zeros_like(acc)
    norm_acc[...] = jnp.zeros_like(norm_acc)
    kin_acc[...] = jnp.zeros_like(kin_acc)
    for index in parts:
        ahead(0, 0, index)
    for index in parts:
        ahead(1, 1, index)
        update(0, 0, index)

    def body(pair, carry):
        for offset in (1, 2):
            step, slot = 2 * pair + offset, offset % 2
            for index in parts:
                ahead(step + 1, 1 - slot, index)
                if index % DEEP == 0:
                    gather(step - 1, 1 - slot, index)
                update(step, slot, index)
        return carry

    lax.fori_loop(0, steps // 2 - 1, body, 0)
    for index in parts:
        if index % DEEP == 0:
            gather(steps - 2, 0, index)
        update(steps - 1, 1, index)
    for index in range(0, count, DEEP):
        gather(steps - 1, 1, index)
    pack_partials(core, acc, stat_rows(norm_acc, kin_acc), own, other)


def last_kernel(
    chunk, core_ref, mine, theirs, band_kin, norm_inv, current, proj, kin, factor,
    out, weight, shift, near_a, near_b, bufs, sems,
):
    core = core_ref[0]
    bands = current.shape[1]
    count = chunk // LANES
    steps = current.shape[0] // count
    nears = (near_a, near_b)
    gather_weights(core, mine, theirs, band_kin, norm_inv, weight, shift)

    piece = chunk // SPLIT

    def send(step, part):
        slot = lax.rem(step, BUFFERS)
        span = pl.ds(pl.multiple_of(step * chunk + part * piece, LANES), piece)
        return pltpu.make_async_copy(
            bufs.at[slot, :, part * piece : (part + 1) * piece], out.at[:, span],
            sems.at[slot, part],
        )

    def ahead(step, side, index):
        nears[side][:, index * LANES : (index + WIDE) * LANES] = jnp.dot(
            weight[...], tiles(proj, step * count + index, WIDE), preferred_element_type=F32
        )

    def update(step, side, first):
        slot = lax.rem(step, BUFFERS)
        for row in range(0, bands, ROWS):
            for index in range(first, first + WIDE):
                kinetic = kinetic_tile(kin, step * count + index)
                bufs[slot, row : row + ROWS, index * LANES : (index + 1) * LANES] = moved(
                    current, kinetic, factor, shift, nears[side], step, count, row, index
                )

    parts = range(0, count, WIDE)
    for index in parts:
        ahead(0, 0, index)

    def body(pair, carry):
        for side in range(2):
            step = 2 * pair + side

            @pl.when(step >= BUFFERS)
            def _():
                for part in range(SPLIT):
                    send(step - BUFFERS, part).wait()

            for index in parts:
                ahead(jnp.minimum(step + 1, steps - 1), 1 - side, index)
                update(step, side, index)
                if (index + WIDE) * LANES % piece == 0:
                    send(step, (index + WIDE) * LANES // piece - 1).start()
        return carry

    lax.fori_loop(0, steps // 2, body, 0)
    for step in range(max(0, steps - BUFFERS), steps):
        for part in range(SPLIT):
            send(step, part).wait()


VM = pl.BlockSpec(memory_space=pltpu.VMEM)
SM = pl.BlockSpec(memory_space=pltpu.SMEM)
HB = pl.BlockSpec(memory_space=pltpu.HBM)


def params(mib):
    return pltpu.CompilerParams(vmem_limit_bytes=mib * MIB)


def swap(value, axis, mask):
    count = lax.axis_size(axis)
    return lax.ppermute(value, axis, [(i, i ^ mask) for i in range(count)])


def masks_direct(count, first):
    return [mask for mask in (first, 2 * first, 3 * first) if mask < count]


def local(
    wave_coeffs, projectors, miller_index, occupations, species_map, proj_counts, onsite_base
):
    bands, plane = wave_coeffs.shape
    slots = projectors.shape[0]
    half = slots // 2
    bands_all = bands * lax.axis_size("gy")
    core = (lax.axis_index("gx") % 2).astype(jnp.int32).reshape(1)
    rows = bands + ROWS
    chunk_first = min(CHUNK_FIRST, plane // 2)
    chunk_middle = min(CHUNK_MIDDLE, plane // 4)
    chunk_last = min(CHUNK_LAST, plane // 4)
    chunk_factor = min(1024, plane)
    def partial_out(kind):
        return (pltpu.VMEM((rows, half), F32), pltpu.VMEM((rows, half), kind))

    stay = functools.partial(pltpu.with_memory_space_constraint, memory_space=pltpu.HBM)
    count = plane // LANES
    flight = max(2, FLIGHT_BYTES // (2 * (bands + slots) * chunk_first))
    band_tiles = pltpu.VMEM((count, bands, LANES), BF16)
    current, proj, kin, live, base, occ, own, other = pl.pallas_call(
        functools.partial(first_kernel, chunk_first, flight),
        out_shape=(
            band_tiles,
            pltpu.VMEM((count, slots, LANES), BF16),
            pltpu.VMEM((PMAX, plane), F32),
            pltpu.VMEM((PMAX, half), F32),
            pltpu.VMEM((PMAX, half), F32),
            pltpu.VMEM((bands, LANES), F32),
        )
        + partial_out(F32),
        in_specs=[SM] + [HB] * 7,
        out_specs=[VM] * 8,
        scratch_shapes=[
            pltpu.VMEM((flight, bands, chunk_first), BF16),
            pltpu.VMEM((flight, slots, chunk_first), BF16),
        ]
        + [pltpu.VMEM((bands, slots), F32)]
        + [pltpu.VMEM((bands, LANES), F32)] * 2
        + [
            pltpu.VMEM(miller_index.shape, jnp.int32),
            pltpu.VMEM((1, bands), F32),
            pltpu.VMEM(onsite_base.shape, F32),
            pltpu.SMEM(species_map.shape, jnp.int32),
            pltpu.SMEM(proj_counts.shape, jnp.int32),
            pltpu.SemaphoreType.DMA((2, flight)),
            pltpu.SemaphoreType.DMA((5,)),
        ],
        compiler_params=params(12),
    )(
        core, stay(wave_coeffs), stay(projectors), stay(miller_index),
        stay(occupations.reshape(1, bands)), stay(onsite_base), stay(species_map),
        stay(proj_counts),
    )
    for turn in range(ITERS):
        came = swap(other, "gx", 1)
        first = 2
        while True:
            total, sent = pl.pallas_call(
                pair_kernel,
                out_shape=partial_out(F32 if turn + 1 < ITERS else BF16),
                in_specs=[VM, VM],
                out_specs=[VM, VM],
                compiler_params=params(4),
            )(own, came)
            arrived = [swap(sent, "gx", m) for m in masks_direct(lax.axis_size("gx"), first)]
            first *= 4
            if first >= lax.axis_size("gx"):
                break
            own = total
            came = sum(part.astype(F32) for part in arrived)
        masked, density, scale, band_kin, norm_inv = pl.pallas_call(
            functools.partial(density_kernel, len(arrived)),
            out_shape=(
                pltpu.VMEM((bands, half), F32),
                pltpu.VMEM((PMAX, half), F32),
                pltpu.VMEM((bands, LANES), F32),
                pltpu.VMEM((bands, LANES), F32),
                pltpu.VMEM((bands, LANES), F32),
            ),
            in_specs=[VM] * (3 + len(arrived)),
            out_specs=[VM] * 5,
            scratch_shapes=[pltpu.VMEM((ROWS, bands), F32)],
            compiler_params=params(10),
        )(total, *arrived, live, occ)
        others = [swap(density, "gy", m) for m in masks_direct(lax.axis_size("gy"), 1)]
        first = 4
        while first < lax.axis_size("gy"):
            density = density + sum(others)
            others = [swap(density, "gy", m) for m in masks_direct(lax.axis_size("gy"), first)]
            first *= 4
        factor_steps = plane // chunk_factor
        turning = factor_steps * SHARE // 16
        begun, done = pl.pallas_call(
            functools.partial(factor_kernel, chunk_factor, 0, turning),
            out_shape=(pltpu.VMEM(wave_coeffs.shape, F32), pltpu.VMEM((PMAX, LANES), F32)),
            in_specs=[VM, VM],
            out_specs=[VM, VM],
            compiler_params=params(4),
            cost_estimate=pl.CostEstimate(
                flops=12 * bands * plane, bytes_accessed=4 * bands * plane, transcendentals=0
            ),
        )(kin, scale)
        mine = pl.pallas_call(
            functools.partial(weight_kernel, len(others), bands_all),
            out_shape=pltpu.VMEM((bands, half + LANES), BF16),
            in_specs=[VM] * (5 + len(others)),
            out_specs=VM,
            scratch_shapes=[pltpu.VMEM((half, half), F32)],
            compiler_params=params(6),
        )(density, *others, masked, live, base, done)
        theirs = swap(mine, "gx", 1)
        factor = pl.pallas_call(
            functools.partial(factor_rest_kernel, chunk_factor, turning, factor_steps),
            out_shape=pltpu.VMEM(wave_coeffs.shape, F32),
            in_specs=[VM] * 4,
            out_specs=VM,
            input_output_aliases={0: 0},
            compiler_params=params(4),
            cost_estimate=pl.CostEstimate(
                flops=12 * bands * plane, bytes_accessed=4 * bands * plane, transcendentals=0
            ),
        )(begun, kin, scale, mine)
        held = (core, mine, theirs, band_kin, norm_inv, current, proj, kin, factor)
        gathered = [
            pltpu.VMEM((bands, slots), BF16),
            pltpu.VMEM((bands, LANES), F32),
        ]
        if turn + 1 < ITERS:
            current, own, other = pl.pallas_call(
                functools.partial(middle_kernel, chunk_middle),
                out_shape=(band_tiles,)
                + partial_out(F32 if turn + 2 < ITERS else BF16),
                in_specs=[SM] + [VM] * 8,
                out_specs=[VM] * 3,
                scratch_shapes=gathered
                + [pltpu.VMEM((bands, slots), F32)]
                + [pltpu.VMEM((bands, LANES), F32)] * 2
                + [pltpu.VMEM((bands, chunk_middle), F32)] * 2
                + [pltpu.VMEM((chunk_middle // LANES, bands, LANES), BF16)] * 2,
                compiler_params=params(13),
            )(*held)
    return pl.pallas_call(
        functools.partial(last_kernel, chunk_last),
        out_shape=jax.ShapeDtypeStruct(wave_coeffs.shape, F32),
        in_specs=[SM] + [VM] * 8,
        out_specs=HB,
        scratch_shapes=gathered
        + [pltpu.VMEM((bands, chunk_last), F32)] * 2
        + [pltpu.VMEM((BUFFERS, bands, chunk_last), F32), pltpu.SemaphoreType.DMA((BUFFERS, SPLIT))],
        compiler_params=params(11),
    )(*held)


def solution(mesh):
    placed = (P("gy", "gx"), P(None, "gx"), P(None, "gx"), P("gy"), P(), P(), P())
    return jax.shard_map(
        local, mesh=mesh, in_specs=placed, out_specs=P("gy", "gx"), check_vma=False
    )
```

```python
import functools

import jax
import jax.numpy as jnp
from jax import lax
from jax.experimental import pallas as pl
from jax.experimental.pallas import tpu as pltpu
from jax.sharding import PartitionSpec as P

PMAX = 8
ITERS = 2
LANES = 128
MIB = 1 << 20
WIDE = 2
NEARS = 4
DEEP = 16
FLIGHT_BYTES = 6 * MIB
BUFFERS = 2
SPLIT = 8
SHARE = 11
CHUNK_FIRST = 2048
CHUNK_MIDDLE = 4096
CHUNK_LAST = 4096
ROWS = 16
STATS = 4
F32 = jnp.float32
BF16 = jnp.bfloat16
HIGH = lax.Precision.HIGHEST


kinetic_unit = 1.0 / 600.0
hubbard_weight = 2.0
step_length = 0.5

NT = (((1,), (1,)), ((), ()))
TN = (((0,), (0,)), ((), ()))


def stat_slots(bands, half):
    return -(-bands // half)


def column_of(rows, first, last):
    pick = lax.broadcasted_iota(jnp.int32, (ROWS, LANES), 0)
    ones = jnp.where((pick >= first) & (pick < last), 1.0, 0.0).astype(F32)
    return lax.dot_general(rows, ones, TN, precision=HIGH, preferred_element_type=F32)


def whole_rows(stats):
    row = lax.broadcasted_iota(jnp.int32, stats.shape, 0)
    return jnp.where(row % 2 == 0, stats + pltpu.roll(stats, ROWS - 1, 0), 0.0)


def split_rows(stats):
    head = stats.astype(BF16).astype(F32)
    rest = pltpu.roll(stats - head, 1, 0)
    row = lax.broadcasted_iota(jnp.int32, stats.shape, 0)
    return jnp.where(row % 2 == 0, head, rest).astype(BF16)


def rows_for(stats, kind):
    return split_rows(stats) if kind == BF16 else stats


def pack_partials(core, acc, stats, own, other):
    bands = acc.shape[0]
    half = own.shape[1]
    kind = other.dtype
    own[0:bands, :] = acc[:, pl.ds(pl.multiple_of(core * half, LANES), half)]
    other[0:bands, :] = acc[:, pl.ds(pl.multiple_of((1 - core) * half, LANES), half)].astype(kind)
    row = lax.broadcasted_iota(jnp.int32, stats.shape, 0)
    stats = whole_rows(jnp.where(row < 2, stats, 2.0 * stats))
    at = bands
    own[at : at + ROWS, :] = jnp.zeros((ROWS, half), F32)
    for slot in range(stat_slots(bands, half)):
        width = min(half, bands - slot * half)
        lift = slice(STATS * slot, STATS * (slot + 1))
        lifted = pltpu.roll(stats, STATS * slot, 0) if slot else stats
        own[at + lift.start : at + lift.stop, 0:width] = lifted[
            lift, slot * half : slot * half + width
        ]
    other[at : at + ROWS, :] = rows_for(own[at : at + ROWS, :], kind)


def stat_rows(norm_acc, kin_acc):
    row = lax.broadcasted_iota(jnp.int32, (ROWS, LANES), 0)
    return lax.dot_general(
        jnp.where(row == 0, 1.0, 0.0).astype(F32), norm_acc[...], NT, precision=HIGH,
        preferred_element_type=F32,
    ) + lax.dot_general(
        jnp.where(row == 2, 1.0, 0.0).astype(F32), kin_acc[...], NT, precision=HIGH,
        preferred_element_type=F32,
    )


def tiles(ref, first, count):
    return jnp.concatenate([ref[first + index] for index in range(count)], axis=1)


def first_kernel(
    chunk, flight, core_ref, wave, proj, miller, occ, base, species_hbm, counts_hbm,
    bands_out, proj_out, kin_out, live_out, base_out, occ_out, own, other,
    wave_buf, proj_buf, acc, norm_acc, kin_acc, miller_buf, occ_buf, base_buf, species, counts, sems, small_sems,
):
    core = core_ref[0]
    bands, plane = wave.shape
    steps = plane // chunk
    count = chunk // LANES
    half = own.shape[1]
    small = [
        pltpu.make_async_copy(source, target, small_sems.at[index])
        for index, (source, target) in enumerate(
            (
                (miller, miller_buf),
                (occ, occ_buf),
                (base, base_buf),
                (species_hbm, species),
                (counts_hbm, counts),
            )
        )
    ]
    for copy in small:
        copy.start()

    def copies(step):
        span = pl.ds(step * chunk, chunk)
        slot = step % flight
        return (
            pltpu.make_async_copy(wave.at[:, span], wave_buf.at[slot], sems.at[0, slot]),
            pltpu.make_async_copy(proj.at[:, span], proj_buf.at[slot], sems.at[1, slot]),
        )

    for step in range(min(flight, steps)):
        for copy in copies(step):
            copy.start()
    acc[...] = jnp.zeros_like(acc)
    norm_acc[...] = jnp.zeros_like(norm_acc)
    kin_acc[...] = jnp.zeros_like(kin_acc)
    for copy in small:
        copy.wait()

    lane = lax.broadcasted_iota(jnp.int32, (PMAX, half), 1)
    slot = lane % PMAX
    atom = lane // PMAX
    atoms_half = half // PMAX

    def tables(index, held):
        count_row, kind_row = held
        here = atom == index
        source = core * atoms_half + index
        return (
            jnp.where(here, counts[source], count_row),
            jnp.where(here, species[source], kind_row),
        )

    zero = jnp.zeros((PMAX, half), jnp.int32)
    count_row, kind_row = lax.fori_loop(0, atoms_half, tables, (zero, zero))
    live_out[...] = jnp.where(slot < count_row, 1.0, 0.0).astype(F32)
    spread = jnp.where(
        lane == lane // PMAX * PMAX + lax.broadcasted_iota(jnp.int32, (PMAX, half), 0), 1.0, 0.0
    ).astype(F32)
    table = jnp.zeros((PMAX, half), F32)
    for kind in range(base.shape[0]):
        block = base_buf[kind]
        symmetric = 0.5 * (
            lax.dot_general(
                block, spread, (((1,), (0,)), ((), ())), precision=HIGH, preferred_element_type=F32
            )
            + lax.dot_general(block, spread, TN, precision=HIGH, preferred_element_type=F32)
        )
        table = jnp.where(kind_row == kind, symmetric, table)
    base_out[...] = table
    occ_rows = jnp.broadcast_to(occ_buf[...], (ROWS, bands))
    occ_out[...] = column_of(occ_rows, 0, 1)

    def step_body(step, carry):
        span = pl.ds(step * chunk, chunk)
        parts = miller_buf[:, span].astype(F32)
        m0, m1, m2 = parts[0:1], parts[1:2], parts[2:3]
        kinetic = (1.5 * m0 * m0 + m1 * m1 + 0.5 * m2 * m2) * kinetic_unit
        halved = jnp.broadcast_to(step_length * kinetic, (PMAX, chunk))
        kin_out[:, span] = halved
        for copy in copies(step):
            copy.wait()
        slot = step % flight
        values = wave_buf[slot]
        others = proj_buf[slot]
        for index in range(count):
            lanes = slice(index * LANES, (index + 1) * LANES)
            bands_out[step * count + index] = values[:, lanes]
            proj_out[step * count + index] = others[:, lanes]
        acc[...] += lax.dot_general(values, others, NT, preferred_element_type=F32)
        for row in range(0, bands, ROWS):
            norm = kin_sum = jnp.zeros((ROWS, LANES), F32)
            for index in range(count):
                lanes = slice(index * LANES, (index + 1) * LANES)
                square = values[row : row + ROWS, lanes].astype(F32)
                square = square * square
                norm = norm + square
                kin_sum = kin_sum + square * jnp.concatenate([halved[:, lanes]] * 2, axis=0)
            norm_acc[row : row + ROWS, :] += norm
            kin_acc[row : row + ROWS, :] += kin_sum

        if step + flight < steps:
            for copy in copies(step + flight):
                copy.start()

        return carry

    for step in range(steps):
        step_body(step, 0)
    pack_partials(core, acc, stat_rows(norm_acc, kin_acc), own, other)


def pair_kernel(own, came, total, sent):
    rows, half = own.shape
    kind = sent.dtype
    value = own[...] + came[...].astype(F32)
    total[...] = value
    sent[...] = value.astype(kind)
    if kind == BF16:
        whole = whole_rows(value[rows - ROWS :])
        total[rows - ROWS :, :] = whole
        sent[rows - ROWS :, :] = split_rows(whole)


def density_kernel(count, *refs):
    total, came = refs[0], refs[1 : 1 + count]
    live, occ, masked, density, rows_buf = refs[1 + count :]
    rows, half = total.shape
    bands = masked.shape[0]
    value = total[...]
    for ref in came:
        value = value + ref[...].astype(F32)
    kept = value[0:bands] * live[0:1, :]
    masked[...] = kept
    full = lax.dot_general(
        kept * occ_wide(occ, half), kept, TN, precision=HIGH, preferred_element_type=F32
    )
    atom = lax.broadcasted_iota(jnp.int32, (PMAX, half), 1) // PMAX
    compact = jnp.zeros((PMAX, half), F32)
    for index in range(half // PMAX):
        block = full[index * PMAX : (index + 1) * PMAX]
        compact = jnp.where(atom == index, block, compact)
    density[...] = compact
    block = value[bands:]
    for slot in range(stat_slots(bands, half)):
        width = min(half, bands - slot * half)
        lowered = pltpu.roll(block, ROWS - STATS * slot, 0) if slot else block
        rows_buf[:, slot * half : slot * half + width] = lowered[:, 0:width]


def occ_wide(occ, half):
    return jnp.concatenate([occ[...]] * (half // LANES), axis=1)


def wide(value, width):
    return jnp.concatenate([value] * (width // LANES), axis=1)


def fill_factor(chunk, first, last, kin, scale, factor):
    bands = factor.shape[0]

    def body(step, carry):
        span = pl.ds(pl.multiple_of(step * chunk, LANES), chunk)
        kinetic = kin[:, span]
        for row in range(0, bands, PMAX):
            y = kinetic * wide(scale[row : row + PMAX, :], chunk)
            square = y * y
            top = (square + 9.0) * (y + 3.0)
            factor[row : row + PMAX, span] = top / (top + square * square)
        return carry

    lax.fori_loop(first, last, body, 0)


def factor_kernel(chunk, first, last, kin, sums, factor, scale, band_kin, norm_inv, done):
    norm = column_of(sums[...], 0, 2)
    mean = column_of(sums[...], 2, 4) / norm
    band_kin[...] = mean
    norm_inv[...] = 1.0 / norm
    scale[...] = 4.0 / mean
    fill_factor(chunk, first, last, kin, scale, factor)
    done[...] = norm[0:PMAX, :]


def factor_rest_kernel(chunk, first, last, begun, kin, scale, after, factor):
    fill_factor(chunk, first, last, kin, scale, factor)


def weight_kernel(count, bands_all, *refs):
    density, came = refs[0], refs[1 : 1 + count]
    masked, live, base, _, out, onsite_buf = refs[1 + count :]
    bands, half = masked.shape
    total = density[...]
    for ref in came:
        total = total + ref[...]
    onsite = base[...] + (hubbard_weight / bands_all) * total
    atom = lax.broadcasted_iota(jnp.int32, (PMAX, half), 1) // PMAX
    for index in range(half // PMAX):
        onsite_buf[index * PMAX : (index + 1) * PMAX, :] = jnp.where(atom == index, onsite, 0.0)
    kept = masked[...]
    weighted = (
        jnp.dot(kept, onsite_buf[...], precision=HIGH, preferred_element_type=F32) * live[0:1, :]
    )
    rounded = weighted.astype(BF16)
    out[:, 0:half] = rounded
    energy = jnp.sum(kept * rounded.astype(F32), axis=1, keepdims=True)
    energy = jnp.broadcast_to(energy, (bands, LANES))
    head = energy.astype(BF16).astype(F32)
    lane = lax.broadcasted_iota(jnp.int32, (bands, LANES), 1)
    packed = jnp.where(lane == 0, head, jnp.where(lane == 1, energy - head, 0.0))
    out[:, half : half + LANES] = packed.astype(BF16)


def gather_weights(core, mine, theirs, band_kin, norm_inv, weight, shift):
    half = mine.shape[1] - LANES
    weight[:, pl.ds(pl.multiple_of(core * half, LANES), half)] = (
        mine[:, 0:half] * jnp.asarray(step_length, BF16)
    )
    weight[:, pl.ds(pl.multiple_of((1 - core) * half, LANES), half)] = (
        theirs[:, 0:half] * jnp.asarray(step_length, BF16)
    )
    parts = mine[:, half : half + LANES].astype(F32) + theirs[:, half : half + LANES].astype(F32)
    energy = jnp.sum(parts, axis=1, keepdims=True)
    shift[...] = step_length * (band_kin[...] + energy * norm_inv[...])


def moved(current, kinetic, factor, shift, near, tile, row, index):
    rows = slice(row, row + ROWS)
    span = pl.ds(pl.multiple_of(tile * LANES, LANES), LANES)
    values = current[tile, rows, :].astype(F32)
    slope = kinetic - shift[rows, :]
    near_here = near[rows, index * LANES : (index + 1) * LANES]
    return values - factor[rows, span] * (slope * values + near_here)


def kinetic_tile(kin, tile):
    row = kin[:, pl.ds(pl.multiple_of(tile * LANES, LANES), LANES)]
    return jnp.concatenate([row] * (ROWS // PMAX), axis=0)


def middle_kernel(
    chunk, core_ref, mine, theirs, band_kin, norm_inv, current, proj, kin, factor,
    following, own, other, weight, shift, acc, norm_acc, kin_acc,
    near_a, near_b, fresh_a, fresh_b,
):
    core = core_ref[0]
    bands = current.shape[1]
    count = chunk // LANES
    deep = min(DEEP, count)
    steps = current.shape[0] // count
    nears, freshes = (near_a, near_b), (fresh_a, fresh_b)
    gather_weights(core, mine, theirs, band_kin, norm_inv, weight, shift)

    def ahead(step, slot, index):
        nears[slot][:, index * LANES : (index + WIDE) * LANES] = jnp.dot(
            weight[...], tiles(proj, step * count + index, WIDE), preferred_element_type=F32
        )

    def update(step, slot, first):
        for row in range(0, bands, ROWS):
            norm = kin_sum = jnp.zeros((ROWS, LANES), F32)
            for index in range(first, first + WIDE):
                kinetic = kinetic_tile(kin, step * count + index)
                value = moved(
                    current, kinetic, factor, shift, nears[slot], step * count + index, row, index
                )
                fresh = value.astype(BF16)
                following[step * count + index, row : row + ROWS, :] = fresh
                freshes[slot][index, row : row + ROWS, :] = fresh
                square = value * value
                norm = norm + square
                kin_sum = kin_sum + square * kinetic
            norm_acc[row : row + ROWS, :] += norm
            kin_acc[row : row + ROWS, :] += kin_sum

    def gather(step, slot, index):
        acc[...] += lax.dot_general(
            tiles(freshes[slot], index, deep), tiles(proj, step * count + index, deep), NT,
            preferred_element_type=F32,
        )

    parts = range(0, count, WIDE)

    acc[...] = jnp.zeros_like(acc)
    norm_acc[...] = jnp.zeros_like(norm_acc)
    kin_acc[...] = jnp.zeros_like(kin_acc)
    for index in parts:
        ahead(0, 0, index)
    for index in parts:
        ahead(1, 1, index)
        update(0, 0, index)

    def body(pair, carry):
        for offset in (1, 2):
            step, slot = 2 * pair + offset, offset % 2
            for index in parts:
                ahead(step + 1, 1 - slot, index)
                if index % deep == 0:
                    gather(step - 1, 1 - slot, index)
                update(step, slot, index)
        return carry

    lax.fori_loop(0, steps // 2 - 1, body, 0)
    for index in parts:
        if index % deep == 0:
            gather(steps - 2, 0, index)
        update(steps - 1, 1, index)
    for index in range(0, count, deep):
        gather(steps - 1, 1, index)
    pack_partials(core, acc, stat_rows(norm_acc, kin_acc), own, other)


def last_kernel(
    chunk, core_ref, mine, theirs, band_kin, norm_inv, current, proj, kin, factor,
    out, weight, shift, nears, bufs, sems,
):
    core = core_ref[0]
    bands = current.shape[1]
    count = chunk // LANES
    steps = current.shape[0] // count
    parts = count // WIDE
    gather_weights(core, mine, theirs, band_kin, norm_inv, weight, shift)

    piece = max(chunk // SPLIT, WIDE * LANES)
    split = chunk // piece

    def send(step, part):
        slot = lax.rem(step, BUFFERS)
        span = pl.ds(pl.multiple_of(step * chunk + part * piece, LANES), piece)
        return pltpu.make_async_copy(
            bufs.at[slot, :, part * piece : (part + 1) * piece], out.at[:, span],
            sems.at[slot, part],
        )

    def ahead(tile, part):
        nears[part % NEARS] = jnp.dot(
            weight[...], tiles(proj, tile, WIDE), preferred_element_type=F32
        )

    def update(tile, part, slot):
        for row in range(0, bands, ROWS):
            for index in range(WIDE):
                kinetic = kinetic_tile(kin, tile + index)
                at = (part * WIDE + index) * LANES
                bufs[slot, row : row + ROWS, at : at + LANES] = moved(
                    current, kinetic, factor, shift, nears.at[part % NEARS], tile + index,
                    row, index,
                )

    ahead(0, 0)

    def body(step, carry):
        slot = lax.rem(step, BUFFERS)

        @pl.when(step >= BUFFERS)
        def _():
            for part in range(split):
                send(step - BUFFERS, part).wait()

        for part in range(parts):
            tile = step * count + part * WIDE
            if part + 1 < parts:
                ahead(tile + WIDE, part + 1)
            else:
                ahead(jnp.minimum(tile + WIDE, (steps - 1) * count), 0)
            update(tile, part, slot)
            if (part + 1) * WIDE * LANES % piece == 0:
                send(step, (part + 1) * WIDE * LANES // piece - 1).start()
        return carry

    lax.fori_loop(0, steps, body, 0)
    for step in range(max(0, steps - BUFFERS), steps):
        for part in range(split):
            send(step, part).wait()


VM = pl.BlockSpec(memory_space=pltpu.VMEM)
SM = pl.BlockSpec(memory_space=pltpu.SMEM)
HB = pl.BlockSpec(memory_space=pltpu.HBM)


def params(mib):
    return pltpu.CompilerParams(vmem_limit_bytes=mib * MIB)


def swap(value, axis, mask):
    count = lax.axis_size(axis)
    return lax.ppermute(value, axis, [(i, i ^ mask) for i in range(count)])


def masks_direct(count, first):
    return [mask for mask in (first, 2 * first, 3 * first) if mask < count]


def local(
    wave_coeffs, projectors, miller_index, occupations, species_map, proj_counts, onsite_base
):
    bands, plane = wave_coeffs.shape
    slots = projectors.shape[0]
    half = slots // 2
    bands_all = bands * lax.axis_size("gy")
    core = (lax.axis_index("gx") % 2).astype(jnp.int32).reshape(1)
    rows = bands + ROWS
    chunk_first = min(CHUNK_FIRST, plane // 2)
    chunk_middle = min(CHUNK_MIDDLE, plane // 4)
    chunk_last = min(CHUNK_LAST, plane // 4)
    chunk_factor = min(1024, plane)
    def partial_out(kind):
        return (pltpu.VMEM((rows, half), F32), pltpu.VMEM((rows, half), kind))

    stay = functools.partial(pltpu.with_memory_space_constraint, memory_space=pltpu.HBM)
    count = plane // LANES
    flight = max(2, FLIGHT_BYTES // (2 * (bands + slots) * chunk_first))
    band_tiles = pltpu.VMEM((count, bands, LANES), BF16)
    current, proj, kin, live, base, occ, own, other = pl.pallas_call(
        functools.partial(first_kernel, chunk_first, flight),
        out_shape=(
            band_tiles,
            pltpu.VMEM((count, slots, LANES), BF16),
            pltpu.VMEM((PMAX, plane), F32),
            pltpu.VMEM((PMAX, half), F32),
            pltpu.VMEM((PMAX, half), F32),
            pltpu.VMEM((bands, LANES), F32),
        )
        + partial_out(F32),
        in_specs=[SM] + [HB] * 7,
        out_specs=[VM] * 8,
        scratch_shapes=[
            pltpu.VMEM((flight, bands, chunk_first), BF16),
            pltpu.VMEM((flight, slots, chunk_first), BF16),
        ]
        + [pltpu.VMEM((bands, slots), F32)]
        + [pltpu.VMEM((bands, LANES), F32)] * 2
        + [
            pltpu.VMEM(miller_index.shape, jnp.int32),
            pltpu.VMEM((1, bands), F32),
            pltpu.VMEM(onsite_base.shape, F32),
            pltpu.SMEM(species_map.shape, jnp.int32),
            pltpu.SMEM(proj_counts.shape, jnp.int32),
            pltpu.SemaphoreType.DMA((2, flight)),
            pltpu.SemaphoreType.DMA((5,)),
        ],
        compiler_params=params(12),
    )(
        core, stay(wave_coeffs), stay(projectors), stay(miller_index),
        stay(occupations.reshape(1, bands)), stay(onsite_base), stay(species_map),
        stay(proj_counts),
    )
    for turn in range(ITERS):
        came = swap(other, "gx", 1)
        first = 2
        while True:
            total, sent = pl.pallas_call(
                pair_kernel,
                out_shape=partial_out(F32 if turn + 1 < ITERS else BF16),
                in_specs=[VM, VM],
                out_specs=[VM, VM],
                compiler_params=params(4),
            )(own, came)
            arrived = [swap(sent, "gx", m) for m in masks_direct(lax.axis_size("gx"), first)]
            first *= 4
            if first >= lax.axis_size("gx"):
                break
            own = total
            came = sum(part.astype(F32) for part in arrived)
        masked, density, sums = pl.pallas_call(
            functools.partial(density_kernel, len(arrived)),
            out_shape=(
                pltpu.VMEM((bands, half), F32),
                pltpu.VMEM((PMAX, half), F32),
                pltpu.VMEM((ROWS, bands), F32),
            ),
            in_specs=[VM] * (3 + len(arrived)),
            out_specs=[VM] * 3,
            compiler_params=params(10),
        )(total, *arrived, live, occ)
        others = [swap(density, "gy", m) for m in masks_direct(lax.axis_size("gy"), 1)]
        first = 4
        while first < lax.axis_size("gy"):
            density = density + sum(others)
            others = [swap(density, "gy", m) for m in masks_direct(lax.axis_size("gy"), first)]
            first *= 4
        factor_steps = plane // chunk_factor
        turning = factor_steps * SHARE // 16
        begun, scale, band_kin, norm_inv, done = pl.pallas_call(
            functools.partial(factor_kernel, chunk_factor, 0, turning),
            out_shape=(pltpu.VMEM(wave_coeffs.shape, F32),)
            + (pltpu.VMEM((bands, LANES), F32),) * 3
            + (pltpu.VMEM((PMAX, LANES), F32),),
            in_specs=[VM, VM],
            out_specs=[VM] * 5,
            compiler_params=params(4),
            cost_estimate=pl.CostEstimate(
                flops=12 * bands * plane, bytes_accessed=4 * bands * plane, transcendentals=0
            ),
        )(kin, sums)
        mine = pl.pallas_call(
            functools.partial(weight_kernel, len(others), bands_all),
            out_shape=pltpu.VMEM((bands, half + LANES), BF16),
            in_specs=[VM] * (5 + len(others)),
            out_specs=VM,
            scratch_shapes=[pltpu.VMEM((half, half), F32)],
            compiler_params=params(6),
        )(density, *others, masked, live, base, done)
        theirs = swap(mine, "gx", 1)
        factor = pl.pallas_call(
            functools.partial(factor_rest_kernel, chunk_factor, turning, factor_steps),
            out_shape=pltpu.VMEM(wave_coeffs.shape, F32),
            in_specs=[VM] * 4,
            out_specs=VM,
            input_output_aliases={0: 0},
            compiler_params=params(4),
            cost_estimate=pl.CostEstimate(
                flops=12 * bands * plane, bytes_accessed=4 * bands * plane, transcendentals=0
            ),
        )(begun, kin, scale, mine)
        held = (core, mine, theirs, band_kin, norm_inv, current, proj, kin, factor)
        gathered = [
            pltpu.VMEM((bands, slots), BF16),
            pltpu.VMEM((bands, LANES), F32),
        ]
        if turn + 1 < ITERS:
            current, own, other = pl.pallas_call(
                functools.partial(middle_kernel, chunk_middle),
                out_shape=(band_tiles,)
                + partial_out(F32 if turn + 2 < ITERS else BF16),
                in_specs=[SM] + [VM] * 8,
                out_specs=[VM] * 3,
                scratch_shapes=gathered
                + [pltpu.VMEM((bands, slots), F32)]
                + [pltpu.VMEM((bands, LANES), F32)] * 2
                + [pltpu.VMEM((bands, chunk_middle), F32)] * 2
                + [pltpu.VMEM((chunk_middle // LANES, bands, LANES), BF16)] * 2,
                compiler_params=params(13),
            )(*held)
    return pl.pallas_call(
        functools.partial(last_kernel, chunk_last),
        out_shape=jax.ShapeDtypeStruct(wave_coeffs.shape, F32),
        in_specs=[SM] + [VM] * 8,
        out_specs=HB,
        scratch_shapes=gathered
        + [pltpu.VMEM((NEARS, bands, WIDE * LANES), F32)]
        + [pltpu.VMEM((BUFFERS, bands, chunk_last), F32), pltpu.SemaphoreType.DMA((BUFFERS, SPLIT))],
        compiler_params=params(11),
    )(*held)


def solution(mesh):
    placed = (P("gy", "gx"), P(None, "gx"), P(None, "gx"), P("gy"), P(), P(), P())
    return jax.shard_map(
        local, mesh=mesh, in_specs=placed, out_specs=P("gy", "gx"), check_vma=False
    )
```

```python
import functools

import jax
import jax.numpy as jnp
from jax import lax
from jax.experimental import pallas as pl
from jax.experimental.pallas import tpu as pltpu
from jax.sharding import PartitionSpec as P

PMAX = 8
ITERS = 2
LANES = 128
MIB = 1 << 20
WIDE = 2
WIDE_LAST = 4
NEARS = 4
DEEP = 16
FLIGHT_BYTES = 6 * MIB
BUFFERS = 2
SPLIT = 8
SHARE = 12
CHUNK_FIRST = 2048
CHUNK_MIDDLE = 4096
CHUNK_LAST = 4096
ROWS = 16
STATS = 4
F32 = jnp.float32
BF16 = jnp.bfloat16
HIGH = lax.Precision.HIGHEST


kinetic_unit = 1.0 / 600.0
hubbard_weight = 2.0
step_length = 0.5

NT = (((1,), (1,)), ((), ()))
TN = (((0,), (0,)), ((), ()))


def stat_slots(bands, half):
    return -(-bands // half)


def column_of(rows, first, last):
    pick = lax.broadcasted_iota(jnp.int32, (ROWS, LANES), 0)
    ones = jnp.where((pick >= first) & (pick < last), 1.0, 0.0).astype(F32)
    return lax.dot_general(rows, ones, TN, precision=HIGH, preferred_element_type=F32)


def whole_rows(stats):
    row = lax.broadcasted_iota(jnp.int32, stats.shape, 0)
    return jnp.where(row % 2 == 0, stats + pltpu.roll(stats, ROWS - 1, 0), 0.0)


def split_rows(stats):
    head = stats.astype(BF16).astype(F32)
    rest = pltpu.roll(stats - head, 1, 0)
    row = lax.broadcasted_iota(jnp.int32, stats.shape, 0)
    return jnp.where(row % 2 == 0, head, rest).astype(BF16)


def rows_for(stats, kind):
    return split_rows(stats) if kind == BF16 else stats


def pack_partials(core, acc, stats, own, other):
    bands = acc.shape[0]
    half = own.shape[1]
    kind = other.dtype
    own[0:bands, :] = acc[:, pl.ds(pl.multiple_of(core * half, LANES), half)]
    other[0:bands, :] = acc[:, pl.ds(pl.multiple_of((1 - core) * half, LANES), half)].astype(kind)
    row = lax.broadcasted_iota(jnp.int32, stats.shape, 0)
    stats = whole_rows(jnp.where(row < 2, stats, 2.0 * stats))
    at = bands
    own[at : at + ROWS, :] = jnp.zeros((ROWS, half), F32)
    for slot in range(stat_slots(bands, half)):
        width = min(half, bands - slot * half)
        lift = slice(STATS * slot, STATS * (slot + 1))
        lifted = pltpu.roll(stats, STATS * slot, 0) if slot else stats
        own[at + lift.start : at + lift.stop, 0:width] = lifted[
            lift, slot * half : slot * half + width
        ]
    other[at : at + ROWS, :] = rows_for(own[at : at + ROWS, :], kind)


def plus(total, term):
    return term if total is None else total + term


def stat_rows(norm_acc, kin_acc):
    row = lax.broadcasted_iota(jnp.int32, (ROWS, LANES), 0)
    return lax.dot_general(
        jnp.where(row == 0, 1.0, 0.0).astype(F32), norm_acc[...], NT, precision=HIGH,
        preferred_element_type=F32,
    ) + lax.dot_general(
        jnp.where(row == 2, 1.0, 0.0).astype(F32), kin_acc[...], NT, precision=HIGH,
        preferred_element_type=F32,
    )


def tiles(ref, first, count):
    return jnp.concatenate([ref[first + index] for index in range(count)], axis=1)


def first_kernel(
    chunk, flight, core_ref, wave, proj, miller, occ, base, species_hbm, counts_hbm,
    bands_out, proj_out, kin_out, live_out, base_out, occ_out, own, other,
    wave_buf, proj_buf, acc, norm_acc, kin_acc, miller_buf, occ_buf, base_buf, species, counts, sems, small_sems,
):
    core = core_ref[0]
    bands, plane = wave.shape
    steps = plane // chunk
    count = chunk // LANES
    half = own.shape[1]
    small = [
        pltpu.make_async_copy(source, target, small_sems.at[index])
        for index, (source, target) in enumerate(
            (
                (miller, miller_buf),
                (occ, occ_buf),
                (base, base_buf),
                (species_hbm, species),
                (counts_hbm, counts),
            )
        )
    ]
    for copy in small:
        copy.start()

    def copies(step):
        span = pl.ds(step * chunk, chunk)
        slot = step % flight
        return (
            pltpu.make_async_copy(wave.at[:, span], wave_buf.at[slot], sems.at[0, slot]),
            pltpu.make_async_copy(proj.at[:, span], proj_buf.at[slot], sems.at[1, slot]),
        )

    for step in range(min(flight, steps)):
        for copy in copies(step):
            copy.start()
    acc[...] = jnp.zeros_like(acc)
    norm_acc[...] = jnp.zeros_like(norm_acc)
    kin_acc[...] = jnp.zeros_like(kin_acc)
    for copy in small:
        copy.wait()

    lane = lax.broadcasted_iota(jnp.int32, (PMAX, half), 1)
    slot = lane % PMAX
    atom = lane // PMAX
    atoms_half = half // PMAX

    def tables(index, held):
        count_row, kind_row = held
        here = atom == index
        source = core * atoms_half + index
        return (
            jnp.where(here, counts[source], count_row),
            jnp.where(here, species[source], kind_row),
        )

    zero = jnp.zeros((PMAX, half), jnp.int32)
    count_row, kind_row = lax.fori_loop(0, atoms_half, tables, (zero, zero))
    live_out[...] = jnp.where(slot < count_row, 1.0, 0.0).astype(F32)
    spread = jnp.where(
        lane == lane // PMAX * PMAX + lax.broadcasted_iota(jnp.int32, (PMAX, half), 0), 1.0, 0.0
    ).astype(F32)
    table = jnp.zeros((PMAX, half), F32)
    for kind in range(base.shape[0]):
        block = base_buf[kind]
        symmetric = 0.5 * (
            lax.dot_general(
                block, spread, (((1,), (0,)), ((), ())), precision=HIGH, preferred_element_type=F32
            )
            + lax.dot_general(block, spread, TN, precision=HIGH, preferred_element_type=F32)
        )
        table = jnp.where(kind_row == kind, symmetric, table)
    base_out[...] = table
    occ_rows = jnp.broadcast_to(occ_buf[...], (ROWS, bands))
    occ_out[...] = column_of(occ_rows, 0, 1)

    def step_body(step, carry):
        span = pl.ds(step * chunk, chunk)
        parts = miller_buf[:, span].astype(F32)
        m0, m1, m2 = parts[0:1], parts[1:2], parts[2:3]
        kinetic = (1.5 * m0 * m0 + m1 * m1 + 0.5 * m2 * m2) * kinetic_unit
        halved = jnp.broadcast_to(step_length * kinetic, (PMAX, chunk))
        kin_out[:, span] = halved
        for copy in copies(step):
            copy.wait()
        slot = step % flight
        values = wave_buf[slot]
        others = proj_buf[slot]
        for index in range(count):
            lanes = slice(index * LANES, (index + 1) * LANES)
            bands_out[step * count + index] = values[:, lanes]
            proj_out[step * count + index] = others[:, lanes]
        acc[...] += lax.dot_general(values, others, NT, preferred_element_type=F32)
        for row in range(0, bands, ROWS):
            norm = kin_sum = None
            for index in range(count):
                lanes = slice(index * LANES, (index + 1) * LANES)
                square = values[row : row + ROWS, lanes].astype(F32)
                square = square * square
                norm = plus(norm, square)
                kin_sum = plus(
                    kin_sum, square * jnp.concatenate([halved[:, lanes]] * 2, axis=0)
                )
            norm_acc[row : row + ROWS, :] += norm
            kin_acc[row : row + ROWS, :] += kin_sum

        if step + flight < steps:
            for copy in copies(step + flight):
                copy.start()

        return carry

    for step in range(steps):
        step_body(step, 0)
    pack_partials(core, acc, stat_rows(norm_acc, kin_acc), own, other)


def pair_kernel(own, came, total, sent):
    rows, half = own.shape
    kind = sent.dtype
    value = own[...] + came[...].astype(F32)
    total[...] = value
    sent[...] = value.astype(kind)
    if kind == BF16:
        whole = whole_rows(value[rows - ROWS :])
        total[rows - ROWS :, :] = whole
        sent[rows - ROWS :, :] = split_rows(whole)


def density_kernel(count, *refs):
    total, came = refs[0], refs[1 : 1 + count]
    live, occ, masked, density, rows_buf = refs[1 + count :]
    rows, half = total.shape
    bands = masked.shape[0]
    value = total[...]
    for ref in came:
        value = value + ref[...].astype(F32)
    kept = value[0:bands] * live[0:1, :]
    masked[...] = kept
    full = lax.dot_general(
        kept * occ_wide(occ, half), kept, TN, precision=HIGH, preferred_element_type=F32
    )
    atom = lax.broadcasted_iota(jnp.int32, (PMAX, half), 1) // PMAX
    compact = jnp.zeros((PMAX, half), F32)
    for index in range(half // PMAX):
        block = full[index * PMAX : (index + 1) * PMAX]
        compact = jnp.where(atom == index, block, compact)
    density[...] = compact
    block = value[bands:]
    for slot in range(stat_slots(bands, half)):
        width = min(half, bands - slot * half)
        lowered = pltpu.roll(block, ROWS - STATS * slot, 0) if slot else block
        rows_buf[:, slot * half : slot * half + width] = lowered[:, 0:width]


def occ_wide(occ, half):
    return jnp.concatenate([occ[...]] * (half // LANES), axis=1)


def wide(value, width):
    return jnp.concatenate([value] * (width // LANES), axis=1)


def fill_factor(chunk, first, last, kin, scale, factor):
    bands = factor.shape[0]

    def body(step, carry):
        span = pl.ds(pl.multiple_of(step * chunk, LANES), chunk)
        kinetic = kin[:, span]
        for row in range(0, bands, PMAX):
            y = kinetic * wide(scale[row : row + PMAX, :], chunk)
            square = y * y
            top = (square + 9.0) * (y + 3.0)
            factor[row : row + PMAX, span] = top / (top + square * square)
        return carry

    lax.fori_loop(first, last, body, 0)


def factor_kernel(chunk, first, last, kin, sums, factor, scale, band_kin, norm_inv, done):
    pick = lax.broadcasted_iota(jnp.int32, (ROWS, 2 * LANES), 0)
    side = lax.broadcasted_iota(jnp.int32, (ROWS, 2 * LANES), 1) // LANES
    both = lax.dot_general(
        sums[...], jnp.where(pick // 2 == side, 1.0, 0.0).astype(F32), TN, precision=HIGH,
        preferred_element_type=F32,
    )
    norm = both[:, 0:LANES]
    mean = both[:, LANES:] / norm
    band_kin[...] = mean
    norm_inv[...] = 1.0 / norm
    scale[...] = 4.0 / mean
    fill_factor(chunk, first, last, kin, scale, factor)
    done[...] = norm[0:PMAX, :]


def factor_rest_kernel(chunk, first, last, begun, kin, scale, after, factor):
    fill_factor(chunk, first, last, kin, scale, factor)


def weight_kernel(count, bands_all, *refs):
    density, came = refs[0], refs[1 : 1 + count]
    masked, live, base, _, out, onsite_buf = refs[1 + count :]
    bands, half = masked.shape
    total = density[...]
    for ref in came:
        total = total + ref[...]
    onsite = base[...] + (hubbard_weight / bands_all) * total
    atom = lax.broadcasted_iota(jnp.int32, (PMAX, half), 1) // PMAX
    for index in range(half // PMAX):
        onsite_buf[index * PMAX : (index + 1) * PMAX, :] = jnp.where(atom == index, onsite, 0.0)
    kept = masked[...]
    weighted = (
        jnp.dot(kept, onsite_buf[...], precision=HIGH, preferred_element_type=F32) * live[0:1, :]
    )
    rounded = weighted.astype(BF16)
    out[:, 0:half] = rounded
    energy = jnp.sum(kept * rounded.astype(F32), axis=1, keepdims=True)
    energy = jnp.broadcast_to(energy, (bands, LANES))
    head = energy.astype(BF16).astype(F32)
    lane = lax.broadcasted_iota(jnp.int32, (bands, LANES), 1)
    packed = jnp.where(lane == 0, head, jnp.where(lane == 1, energy - head, 0.0))
    out[:, half : half + LANES] = packed.astype(BF16)


def gather_weights(core, mine, theirs, band_kin, norm_inv, weight, shift):
    half = mine.shape[1] - LANES
    weight[:, pl.ds(pl.multiple_of(core * half, LANES), half)] = (
        mine[:, 0:half] * jnp.asarray(step_length, BF16)
    )
    weight[:, pl.ds(pl.multiple_of((1 - core) * half, LANES), half)] = (
        theirs[:, 0:half] * jnp.asarray(step_length, BF16)
    )
    parts = mine[:, half : half + LANES].astype(F32) + theirs[:, half : half + LANES].astype(F32)
    energy = jnp.sum(parts, axis=1, keepdims=True)
    shift[...] = step_length * (band_kin[...] + energy * norm_inv[...])


def moved(current, kinetic, factor, shift, near, tile, row, index):
    rows = slice(row, row + ROWS)
    span = pl.ds(pl.multiple_of(tile * LANES, LANES), LANES)
    values = current[tile, rows, :].astype(F32)
    slope = kinetic - shift[rows, :]
    near_here = near[rows, index * LANES : (index + 1) * LANES]
    return values - factor[rows, span] * (slope * values + near_here)


def kinetic_tile(kin, tile):
    row = kin[:, pl.ds(pl.multiple_of(tile * LANES, LANES), LANES)]
    return jnp.concatenate([row] * (ROWS // PMAX), axis=0)


def middle_kernel(
    chunk, core_ref, mine, theirs, band_kin, norm_inv, current, proj, kin, factor,
    following, own, other, weight, shift, acc, norm_acc, kin_acc,
    near_a, near_b, fresh_a, fresh_b,
):
    core = core_ref[0]
    bands = current.shape[1]
    count = chunk // LANES
    deep = min(DEEP, count)
    steps = current.shape[0] // count
    nears, freshes = (near_a, near_b), (fresh_a, fresh_b)
    gather_weights(core, mine, theirs, band_kin, norm_inv, weight, shift)

    def ahead(step, slot, index):
        nears[slot][:, index * LANES : (index + WIDE) * LANES] = jnp.dot(
            weight[...], tiles(proj, step * count + index, WIDE), preferred_element_type=F32
        )

    def update(step, slot, first):
        for row in range(0, bands, ROWS):
            norm = kin_sum = None
            for index in range(first, first + WIDE):
                kinetic = kinetic_tile(kin, step * count + index)
                value = moved(
                    current, kinetic, factor, shift, nears[slot], step * count + index, row, index
                )
                fresh = value.astype(BF16)
                following[step * count + index, row : row + ROWS, :] = fresh
                freshes[slot][index, row : row + ROWS, :] = fresh
                square = value * value
                norm = plus(norm, square)
                kin_sum = plus(kin_sum, square * kinetic)
            norm_acc[row : row + ROWS, :] += norm
            kin_acc[row : row + ROWS, :] += kin_sum

    def gather(step, slot, index):
        acc[...] += lax.dot_general(
            tiles(freshes[slot], index, deep), tiles(proj, step * count + index, deep), NT,
            preferred_element_type=F32,
        )

    parts = range(0, count, WIDE)

    acc[...] = jnp.zeros_like(acc)
    norm_acc[...] = jnp.zeros_like(norm_acc)
    kin_acc[...] = jnp.zeros_like(kin_acc)
    for index in parts:
        ahead(0, 0, index)
    for index in parts:
        ahead(1, 1, index)
        update(0, 0, index)

    def body(pair, carry):
        for offset in (1, 2):
            step, slot = 2 * pair + offset, offset % 2
            for index in parts:
                ahead(step + 1, 1 - slot, index)
                if index % deep == 0:
                    gather(step - 1, 1 - slot, index)
                update(step, slot, index)
        return carry

    lax.fori_loop(0, steps // 2 - 1, body, 0)
    for index in parts:
        if index % deep == 0:
            gather(steps - 2, 0, index)
        update(steps - 1, 1, index)
    for index in range(0, count, deep):
        gather(steps - 1, 1, index)
    pack_partials(core, acc, stat_rows(norm_acc, kin_acc), own, other)


def last_kernel(
    chunk, core_ref, mine, theirs, band_kin, norm_inv, current, proj, kin, factor,
    out, weight, shift, nears, bufs, sems,
):
    core = core_ref[0]
    bands = current.shape[1]
    count = chunk // LANES
    steps = current.shape[0] // count
    parts = count // WIDE_LAST
    gather_weights(core, mine, theirs, band_kin, norm_inv, weight, shift)

    piece = max(chunk // SPLIT, WIDE_LAST * LANES)
    split = chunk // piece

    def send(step, part):
        slot = lax.rem(step, BUFFERS)
        span = pl.ds(pl.multiple_of(step * chunk + part * piece, LANES), piece)
        return pltpu.make_async_copy(
            bufs.at[slot, :, part * piece : (part + 1) * piece], out.at[:, span],
            sems.at[slot, part],
        )

    def ahead(tile, part):
        nears[part % NEARS] = jnp.dot(
            weight[...], tiles(proj, tile, WIDE_LAST), preferred_element_type=F32
        )

    def update(tile, part, slot):
        for row in range(0, bands, ROWS):
            for index in range(WIDE_LAST):
                kinetic = kinetic_tile(kin, tile + index)
                at = (part * WIDE_LAST + index) * LANES
                bufs[slot, row : row + ROWS, at : at + LANES] = moved(
                    current, kinetic, factor, shift, nears.at[part % NEARS], tile + index,
                    row, index,
                )

    ahead(0, 0)

    def body(step, carry):
        slot = lax.rem(step, BUFFERS)

        @pl.when(step >= BUFFERS)
        def _():
            for part in range(split):
                send(step - BUFFERS, part).wait()

        for part in range(parts):
            tile = step * count + part * WIDE_LAST
            if part + 1 < parts:
                ahead(tile + WIDE_LAST, part + 1)
            else:
                ahead(jnp.minimum(tile + WIDE_LAST, (steps - 1) * count), 0)
            update(tile, part, slot)
            if (part + 1) * WIDE_LAST * LANES % piece == 0:
                send(step, (part + 1) * WIDE_LAST * LANES // piece - 1).start()
        return carry

    lax.fori_loop(0, steps, body, 0)
    for step in range(max(0, steps - BUFFERS), steps):
        for part in range(split):
            send(step, part).wait()


VM = pl.BlockSpec(memory_space=pltpu.VMEM)
SM = pl.BlockSpec(memory_space=pltpu.SMEM)
HB = pl.BlockSpec(memory_space=pltpu.HBM)


def params(mib):
    return pltpu.CompilerParams(vmem_limit_bytes=mib * MIB)


def swap(value, axis, mask):
    count = lax.axis_size(axis)
    return lax.ppermute(value, axis, [(i, i ^ mask) for i in range(count)])


def masks_direct(count, first):
    return [mask for mask in (first, 2 * first, 3 * first) if mask < count]


def local(
    wave_coeffs, projectors, miller_index, occupations, species_map, proj_counts, onsite_base
):
    bands, plane = wave_coeffs.shape
    slots = projectors.shape[0]
    half = slots // 2
    bands_all = bands * lax.axis_size("gy")
    core = (lax.axis_index("gx") % 2).astype(jnp.int32).reshape(1)
    rows = bands + ROWS
    chunk_first = min(CHUNK_FIRST, plane // 2)
    chunk_middle = min(CHUNK_MIDDLE, plane // 4)
    chunk_last = min(CHUNK_LAST, plane // 4)
    chunk_factor = min(1024, plane)
    def partial_out(kind):
        return (pltpu.VMEM((rows, half), F32), pltpu.VMEM((rows, half), kind))

    stay = functools.partial(pltpu.with_memory_space_constraint, memory_space=pltpu.HBM)
    count = plane // LANES
    flight = max(2, FLIGHT_BYTES // (2 * (bands + slots) * chunk_first))
    band_tiles = pltpu.VMEM((count, bands, LANES), BF16)
    current, proj, kin, live, base, occ, own, other = pl.pallas_call(
        functools.partial(first_kernel, chunk_first, flight),
        out_shape=(
            band_tiles,
            pltpu.VMEM((count, slots, LANES), BF16),
            pltpu.VMEM((PMAX, plane), F32),
            pltpu.VMEM((PMAX, half), F32),
            pltpu.VMEM((PMAX, half), F32),
            pltpu.VMEM((bands, LANES), F32),
        )
        + partial_out(F32),
        in_specs=[SM] + [HB] * 7,
        out_specs=[VM] * 8,
        scratch_shapes=[
            pltpu.VMEM((flight, bands, chunk_first), BF16),
            pltpu.VMEM((flight, slots, chunk_first), BF16),
        ]
        + [pltpu.VMEM((bands, slots), F32)]
        + [pltpu.VMEM((bands, LANES), F32)] * 2
        + [
            pltpu.VMEM(miller_index.shape, jnp.int32),
            pltpu.VMEM((1, bands), F32),
            pltpu.VMEM(onsite_base.shape, F32),
            pltpu.SMEM(species_map.shape, jnp.int32),
            pltpu.SMEM(proj_counts.shape, jnp.int32),
            pltpu.SemaphoreType.DMA((2, flight)),
            pltpu.SemaphoreType.DMA((5,)),
        ],
        compiler_params=params(12),
    )(
        core, stay(wave_coeffs), stay(projectors), stay(miller_index),
        stay(occupations.reshape(1, bands)), stay(onsite_base), stay(species_map),
        stay(proj_counts),
    )
    for turn in range(ITERS):
        came = swap(other, "gx", 1)
        first = 2
        while True:
            total, sent = pl.pallas_call(
                pair_kernel,
                out_shape=partial_out(F32 if turn + 1 < ITERS else BF16),
                in_specs=[VM, VM],
                out_specs=[VM, VM],
                compiler_params=params(4),
            )(own, came)
            arrived = [swap(sent, "gx", m) for m in masks_direct(lax.axis_size("gx"), first)]
            first *= 4
            if first >= lax.axis_size("gx"):
                break
            own = total
            came = sum(part.astype(F32) for part in arrived)
        masked, density, sums = pl.pallas_call(
            functools.partial(density_kernel, len(arrived)),
            out_shape=(
                pltpu.VMEM((bands, half), F32),
                pltpu.VMEM((PMAX, half), F32),
                pltpu.VMEM((ROWS, bands), F32),
            ),
            in_specs=[VM] * (3 + len(arrived)),
            out_specs=[VM] * 3,
            compiler_params=params(10),
        )(total, *arrived, live, occ)
        others = [swap(density, "gy", m) for m in masks_direct(lax.axis_size("gy"), 1)]
        first = 4
        while first < lax.axis_size("gy"):
            density = density + sum(others)
            others = [swap(density, "gy", m) for m in masks_direct(lax.axis_size("gy"), first)]
            first *= 4
        factor_steps = plane // chunk_factor
        turning = factor_steps * SHARE // 16
        begun, scale, band_kin, norm_inv, done = pl.pallas_call(
            functools.partial(factor_kernel, chunk_factor, 0, turning),
            out_shape=(pltpu.VMEM(wave_coeffs.shape, F32),)
            + (pltpu.VMEM((bands, LANES), F32),) * 3
            + (pltpu.VMEM((PMAX, LANES), F32),),
            in_specs=[VM, VM],
            out_specs=[VM] * 5,
            compiler_params=params(4),
            cost_estimate=pl.CostEstimate(
                flops=12 * bands * plane, bytes_accessed=4 * bands * plane, transcendentals=0
            ),
        )(kin, sums)
        mine = pl.pallas_call(
            functools.partial(weight_kernel, len(others), bands_all),
            out_shape=pltpu.VMEM((bands, half + LANES), BF16),
            in_specs=[VM] * (5 + len(others)),
            out_specs=VM,
            scratch_shapes=[pltpu.VMEM((half, half), F32)],
            compiler_params=params(6),
        )(density, *others, masked, live, base, done)
        theirs = swap(mine, "gx", 1)
        factor = pl.pallas_call(
            functools.partial(factor_rest_kernel, chunk_factor, turning, factor_steps),
            out_shape=pltpu.VMEM(wave_coeffs.shape, F32),
            in_specs=[VM] * 4,
            out_specs=VM,
            input_output_aliases={0: 0},
            compiler_params=params(4),
            cost_estimate=pl.CostEstimate(
                flops=12 * bands * plane, bytes_accessed=4 * bands * plane, transcendentals=0
            ),
        )(begun, kin, scale, mine)
        held = (core, mine, theirs, band_kin, norm_inv, current, proj, kin, factor)
        gathered = [
            pltpu.VMEM((bands, slots), BF16),
            pltpu.VMEM((bands, LANES), F32),
        ]
        if turn + 1 < ITERS:
            current, own, other = pl.pallas_call(
                functools.partial(middle_kernel, chunk_middle),
                out_shape=(band_tiles,)
                + partial_out(F32 if turn + 2 < ITERS else BF16),
                in_specs=[SM] + [VM] * 8,
                out_specs=[VM] * 3,
                scratch_shapes=gathered
                + [pltpu.VMEM((bands, slots), F32)]
                + [pltpu.VMEM((bands, LANES), F32)] * 2
                + [pltpu.VMEM((bands, chunk_middle), F32)] * 2
                + [pltpu.VMEM((chunk_middle // LANES, bands, LANES), BF16)] * 2,
                compiler_params=params(13),
            )(*held)
    return pl.pallas_call(
        functools.partial(last_kernel, chunk_last),
        out_shape=jax.ShapeDtypeStruct(wave_coeffs.shape, F32),
        in_specs=[SM] + [VM] * 8,
        out_specs=HB,
        scratch_shapes=gathered
        + [pltpu.VMEM((NEARS, bands, WIDE_LAST * LANES), F32)]
        + [pltpu.VMEM((BUFFERS, bands, chunk_last), F32), pltpu.SemaphoreType.DMA((BUFFERS, SPLIT))],
        compiler_params=params(11),
    )(*held)


def solution(mesh):
    placed = (P("gy", "gx"), P(None, "gx"), P(None, "gx"), P("gy"), P(), P(), P())
    return jax.shard_map(
        local, mesh=mesh, in_specs=placed, out_specs=P("gy", "gx"), check_vma=False
    )
```

```python
import functools

import jax
import jax.numpy as jnp
from jax import lax
from jax.experimental import pallas as pl
from jax.experimental.pallas import tpu as pltpu
from jax.sharding import PartitionSpec as P

PMAX = 8
ITERS = 2
LANES = 128
MIB = 1 << 20
WIDE = 2
WIDE_LAST = 4
NEARS = 4
DEEP = 16
FLIGHT_BYTES = 6 * MIB
BUFFERS = 2
SPLIT = 8
SHARE = 12
CHUNK_FIRST = 2048
CHUNK_MIDDLE = 4096
CHUNK_LAST = 4096
ROWS = 16
STATS = 4
F32 = jnp.float32
BF16 = jnp.bfloat16
HIGH = lax.Precision.HIGHEST


kinetic_unit = 1.0 / 600.0
hubbard_weight = 2.0
step_length = 0.5

NT = (((1,), (1,)), ((), ()))
TN = (((0,), (0,)), ((), ()))


def stat_slots(bands, half):
    return -(-bands // half)


def column_of(rows, first, last):
    pick = lax.broadcasted_iota(jnp.int32, (ROWS, LANES), 0)
    ones = jnp.where((pick >= first) & (pick < last), 1.0, 0.0).astype(F32)
    return lax.dot_general(rows, ones, TN, precision=HIGH, preferred_element_type=F32)


def whole_rows(stats):
    row = lax.broadcasted_iota(jnp.int32, stats.shape, 0)
    return jnp.where(row % 2 == 0, stats + pltpu.roll(stats, ROWS - 1, 0), 0.0)


def split_rows(stats):
    head = stats.astype(BF16).astype(F32)
    rest = pltpu.roll(stats - head, 1, 0)
    row = lax.broadcasted_iota(jnp.int32, stats.shape, 0)
    return jnp.where(row % 2 == 0, head, rest).astype(BF16)


def rows_for(stats, kind):
    return split_rows(stats) if kind == BF16 else stats


def pack_partials(core, acc, stats, own, other):
    bands = acc.shape[0]
    half = own.shape[1]
    kind = other.dtype
    own[0:bands, :] = acc[:, pl.ds(pl.multiple_of(core * half, LANES), half)]
    other[0:bands, :] = acc[:, pl.ds(pl.multiple_of((1 - core) * half, LANES), half)].astype(kind)
    row = lax.broadcasted_iota(jnp.int32, stats.shape, 0)
    stats = whole_rows(jnp.where(row < 2, stats, 2.0 * stats))
    at = bands
    own[at : at + ROWS, :] = jnp.zeros((ROWS, half), F32)
    for slot in range(stat_slots(bands, half)):
        width = min(half, bands - slot * half)
        lift = slice(STATS * slot, STATS * (slot + 1))
        lifted = pltpu.roll(stats, STATS * slot, 0) if slot else stats
        own[at + lift.start : at + lift.stop, 0:width] = lifted[
            lift, slot * half : slot * half + width
        ]
    other[at : at + ROWS, :] = rows_for(own[at : at + ROWS, :], kind)


def plus(total, term):
    return term if total is None else total + term


def stat_rows(norm_acc, kin_acc):
    row = lax.broadcasted_iota(jnp.int32, (ROWS, LANES), 0)
    return lax.dot_general(
        jnp.where(row == 0, 1.0, 0.0).astype(F32), norm_acc[...], NT, precision=HIGH,
        preferred_element_type=F32,
    ) + lax.dot_general(
        jnp.where(row == 2, 1.0, 0.0).astype(F32), kin_acc[...], NT, precision=HIGH,
        preferred_element_type=F32,
    )


def tiles(ref, first, count):
    return jnp.concatenate([ref[first + index] for index in range(count)], axis=1)


def first_kernel(
    chunk, flight, core_ref, wave, proj, miller, occ, base, species_hbm, counts_hbm,
    bands_out, proj_out, kin_out, live_out, base_out, occ_out, own, other,
    wave_buf, proj_buf, acc, norm_acc, kin_acc, miller_buf, occ_buf, base_buf, species, counts, sems, small_sems,
):
    core = core_ref[0]
    bands, plane = wave.shape
    steps = plane // chunk
    count = chunk // LANES
    half = own.shape[1]
    small = [
        pltpu.make_async_copy(source, target, small_sems.at[index])
        for index, (source, target) in enumerate(
            (
                (miller, miller_buf),
                (occ, occ_buf),
                (base, base_buf),
                (species_hbm, species),
                (counts_hbm, counts),
            )
        )
    ]
    for copy in small:
        copy.start()

    def copies(step):
        span = pl.ds(step * chunk, chunk)
        slot = step % flight
        return (
            pltpu.make_async_copy(wave.at[:, span], wave_buf.at[slot], sems.at[0, slot]),
            pltpu.make_async_copy(proj.at[:, span], proj_buf.at[slot], sems.at[1, slot]),
        )

    for step in range(min(flight, steps)):
        for copy in copies(step):
            copy.start()
    acc[...] = jnp.zeros_like(acc)
    norm_acc[...] = jnp.zeros_like(norm_acc)
    kin_acc[...] = jnp.zeros_like(kin_acc)
    for copy in small:
        copy.wait()

    lane = lax.broadcasted_iota(jnp.int32, (PMAX, half), 1)
    slot = lane % PMAX
    atom = lane // PMAX
    atoms_half = half // PMAX

    def tables(index, held):
        count_row, kind_row = held
        here = atom == index
        source = core * atoms_half + index
        return (
            jnp.where(here, counts[source], count_row),
            jnp.where(here, species[source], kind_row),
        )

    zero = jnp.zeros((PMAX, half), jnp.int32)
    count_row, kind_row = lax.fori_loop(0, atoms_half, tables, (zero, zero))
    live_out[...] = jnp.where(slot < count_row, 1.0, 0.0).astype(F32)
    spread = jnp.where(
        lane == lane // PMAX * PMAX + lax.broadcasted_iota(jnp.int32, (PMAX, half), 0), 1.0, 0.0
    ).astype(F32)
    table = jnp.zeros((PMAX, half), F32)
    for kind in range(base.shape[0]):
        block = base_buf[kind]
        symmetric = 0.5 * (
            lax.dot_general(
                block, spread, (((1,), (0,)), ((), ())), precision=HIGH, preferred_element_type=F32
            )
            + lax.dot_general(block, spread, TN, precision=HIGH, preferred_element_type=F32)
        )
        table = jnp.where(kind_row == kind, symmetric, table)
    base_out[...] = table
    occ_rows = jnp.broadcast_to(occ_buf[...], (ROWS, bands))
    occ_out[...] = column_of(occ_rows, 0, 1)

    def step_body(step, carry):
        span = pl.ds(step * chunk, chunk)
        parts = miller_buf[:, span].astype(F32)
        m0, m1, m2 = parts[0:1], parts[1:2], parts[2:3]
        kinetic = (1.5 * m0 * m0 + m1 * m1 + 0.5 * m2 * m2) * kinetic_unit
        halved = jnp.broadcast_to(step_length * kinetic, (PMAX, chunk))
        kin_out[:, span] = halved
        for copy in copies(step):
            copy.wait()
        slot = step % flight
        values = wave_buf[slot]
        others = proj_buf[slot]
        for index in range(count):
            lanes = slice(index * LANES, (index + 1) * LANES)
            bands_out[step * count + index] = values[:, lanes]
            proj_out[step * count + index] = others[:, lanes]
        acc[...] += lax.dot_general(values, others, NT, preferred_element_type=F32)
        for row in range(0, bands, ROWS):
            norm = kin_sum = None
            for index in range(count):
                lanes = slice(index * LANES, (index + 1) * LANES)
                square = values[row : row + ROWS, lanes].astype(F32)
                square = square * square
                norm = plus(norm, square)
                kin_sum = plus(
                    kin_sum, square * jnp.concatenate([halved[:, lanes]] * 2, axis=0)
                )
            norm_acc[row : row + ROWS, :] += norm
            kin_acc[row : row + ROWS, :] += kin_sum

        if step + flight < steps:
            for copy in copies(step + flight):
                copy.start()

        return carry

    for step in range(steps):
        step_body(step, 0)
    pack_partials(core, acc, stat_rows(norm_acc, kin_acc), own, other)


def pair_kernel(own, came, total, sent):
    rows, half = own.shape
    kind = sent.dtype
    value = own[...] + came[...].astype(F32)
    total[...] = value
    sent[...] = value.astype(kind)
    if kind == BF16:
        whole = whole_rows(value[rows - ROWS :])
        total[rows - ROWS :, :] = whole
        sent[rows - ROWS :, :] = split_rows(whole)


def density_kernel(count, *refs):
    total, came = refs[0], refs[1 : 1 + count]
    live, occ, masked, density, rows_buf = refs[1 + count :]
    rows, half = total.shape
    bands = masked.shape[0]
    value = total[...]
    for ref in came:
        value = value + ref[...].astype(F32)
    kept = value[0:bands] * live[0:1, :]
    masked[...] = kept
    full = lax.dot_general(
        kept * occ_wide(occ, half), kept, TN, precision=HIGH, preferred_element_type=F32
    )
    atom = lax.broadcasted_iota(jnp.int32, (PMAX, half), 1) // PMAX
    compact = jnp.zeros((PMAX, half), F32)
    for index in range(half // PMAX):
        block = full[index * PMAX : (index + 1) * PMAX]
        compact = jnp.where(atom == index, block, compact)
    density[...] = compact
    block = value[bands:]
    for slot in range(stat_slots(bands, half)):
        width = min(half, bands - slot * half)
        lowered = pltpu.roll(block, ROWS - STATS * slot, 0) if slot else block
        rows_buf[:, slot * half : slot * half + width] = lowered[:, 0:width]


def occ_wide(occ, half):
    return jnp.concatenate([occ[...]] * (half // LANES), axis=1)


def wide(value, width):
    return jnp.concatenate([value] * (width // LANES), axis=1)


def fill_factor(chunk, first, last, kin, scale, factor):
    bands = factor.shape[0]

    def body(step, carry):
        span = pl.ds(pl.multiple_of(step * chunk, LANES), chunk)
        kinetic = kin[:, span]
        for row in range(0, bands, PMAX):
            y = kinetic * wide(scale[row : row + PMAX, :], chunk)
            square = y * y
            top = (square + 9.0) * (y + 3.0)
            factor[row : row + PMAX, span] = top / (top + square * square)
        return carry

    lax.fori_loop(first, last, body, 0)


def factor_kernel(chunk, first, last, kin, sums, factor, scale, band_kin, norm_inv, done):
    pick = lax.broadcasted_iota(jnp.int32, (ROWS, 2 * LANES), 0)
    side = lax.broadcasted_iota(jnp.int32, (ROWS, 2 * LANES), 1) // LANES
    both = lax.dot_general(
        sums[...], jnp.where(pick // 2 == side, 1.0, 0.0).astype(F32), TN, precision=HIGH,
        preferred_element_type=F32,
    )
    norm = both[:, 0:LANES]
    mean = both[:, LANES:] / norm
    band_kin[...] = mean
    norm_inv[...] = 1.0 / norm
    scale[...] = 4.0 / mean
    fill_factor(chunk, first, last, kin, scale, factor)
    done[...] = norm[0:PMAX, :]


def factor_rest_kernel(chunk, first, last, begun, kin, scale, after, factor):
    fill_factor(chunk, first, last, kin, scale, factor)


def weight_kernel(count, bands_all, *refs):
    density, came = refs[0], refs[1 : 1 + count]
    masked, live, base, _, out, onsite_buf = refs[1 + count :]
    bands, half = masked.shape
    total = density[...]
    for ref in came:
        total = total + ref[...]
    onsite = base[...] + (hubbard_weight / bands_all) * total
    atom = lax.broadcasted_iota(jnp.int32, (PMAX, half), 1) // PMAX
    for index in range(half // PMAX):
        onsite_buf[index * PMAX : (index + 1) * PMAX, :] = jnp.where(atom == index, onsite, 0.0)
    kept = masked[...]
    weighted = (
        jnp.dot(kept, onsite_buf[...], precision=HIGH, preferred_element_type=F32) * live[0:1, :]
    )
    rounded = weighted.astype(BF16)
    out[:, 0:half] = rounded
    energy = jnp.sum(kept * rounded.astype(F32), axis=1, keepdims=True)
    energy = jnp.broadcast_to(energy, (bands, LANES))
    head = energy.astype(BF16).astype(F32)
    lane = lax.broadcasted_iota(jnp.int32, (bands, LANES), 1)
    packed = jnp.where(lane == 0, head, jnp.where(lane == 1, energy - head, 0.0))
    out[:, half : half + LANES] = packed.astype(BF16)


def gather_weights(core, mine, theirs, band_kin, norm_inv, weight, shift):
    half = mine.shape[1] - LANES
    weight[:, pl.ds(pl.multiple_of(core * half, LANES), half)] = (
        mine[:, 0:half] * jnp.asarray(step_length, BF16)
    )
    weight[:, pl.ds(pl.multiple_of((1 - core) * half, LANES), half)] = (
        theirs[:, 0:half] * jnp.asarray(step_length, BF16)
    )
    parts = mine[:, half : half + LANES].astype(F32) + theirs[:, half : half + LANES].astype(F32)
    energy = jnp.sum(parts, axis=1, keepdims=True)
    shift[...] = step_length * (band_kin[...] + energy * norm_inv[...])


def moved(current, kinetic, factor, shift, near, tile, row, index):
    rows = slice(row, row + ROWS)
    span = pl.ds(pl.multiple_of(tile * LANES, LANES), LANES)
    values = current[tile, rows, :].astype(F32)
    slope = kinetic - shift[rows, :]
    near_here = near[rows, index * LANES : (index + 1) * LANES]
    return values - factor[rows, span] * (slope * values + near_here)


def kinetic_tile(kin, tile):
    row = kin[:, pl.ds(pl.multiple_of(tile * LANES, LANES), LANES)]
    return jnp.concatenate([row] * (ROWS // PMAX), axis=0)


def middle_kernel(
    chunk, core_ref, mine, theirs, band_kin, norm_inv, current, proj, kin, factor,
    following, own, other, weight, shift, acc, norm_acc, kin_acc,
    near_a, near_b, fresh_a, fresh_b,
):
    core = core_ref[0]
    bands = current.shape[1]
    count = chunk // LANES
    deep = min(DEEP, count)
    steps = current.shape[0] // count
    nears, freshes = (near_a, near_b), (fresh_a, fresh_b)
    gather_weights(core, mine, theirs, band_kin, norm_inv, weight, shift)

    def ahead(step, slot, index):
        nears[slot][:, index * LANES : (index + WIDE) * LANES] = jnp.dot(
            weight[...], tiles(proj, step * count + index, WIDE), preferred_element_type=F32
        )

    def update(step, slot, first):
        for row in range(0, bands, ROWS):
            norm = kin_sum = None
            for index in range(first, first + WIDE):
                kinetic = kinetic_tile(kin, step * count + index)
                value = moved(
                    current, kinetic, factor, shift, nears[slot], step * count + index, row, index
                )
                fresh = value.astype(BF16)
                following[step * count + index, row : row + ROWS, :] = fresh
                freshes[slot][index, row : row + ROWS, :] = fresh
                square = value * value
                norm = plus(norm, square)
                kin_sum = plus(kin_sum, square * kinetic)
            norm_acc[row : row + ROWS, :] += norm
            kin_acc[row : row + ROWS, :] += kin_sum

    def gather(step, slot, index):
        acc[...] += lax.dot_general(
            tiles(freshes[slot], index, deep), tiles(proj, step * count + index, deep), NT,
            preferred_element_type=F32,
        )

    parts = range(0, count, WIDE)

    acc[...] = jnp.zeros_like(acc)
    norm_acc[...] = jnp.zeros_like(norm_acc)
    kin_acc[...] = jnp.zeros_like(kin_acc)
    for index in parts:
        ahead(0, 0, index)
    for index in parts:
        ahead(1, 1, index)
        update(0, 0, index)

    def body(pair, carry):
        for offset in (1, 2):
            step, slot = 2 * pair + offset, offset % 2
            for index in parts:
                ahead(step + 1, 1 - slot, index)
                if index % deep == 0:
                    gather(step - 1, 1 - slot, index)
                update(step, slot, index)
        return carry

    lax.fori_loop(0, steps // 2 - 1, body, 0)
    for index in parts:
        if index % deep == 0:
            gather(steps - 2, 0, index)
        update(steps - 1, 1, index)
    for index in range(0, count, deep):
        gather(steps - 1, 1, index)
    pack_partials(core, acc, stat_rows(norm_acc, kin_acc), own, other)


def last_kernel(
    chunk, core_ref, mine, theirs, band_kin, norm_inv, current, proj, kin, factor,
    out, weight, shift, nears, bufs, sems,
):
    core = core_ref[0]
    bands = current.shape[1]
    count = chunk // LANES
    steps = current.shape[0] // count
    parts = count // WIDE_LAST
    gather_weights(core, mine, theirs, band_kin, norm_inv, weight, shift)

    piece = max(chunk // SPLIT, WIDE_LAST * LANES)
    split = chunk // piece

    def send(step, part):
        slot = lax.rem(step, BUFFERS)
        span = pl.ds(pl.multiple_of(step * chunk + part * piece, LANES), piece)
        return pltpu.make_async_copy(
            bufs.at[slot, :, part * piece : (part + 1) * piece], out.at[:, span],
            sems.at[slot, part],
        )

    def ahead(tile, part):
        nears[part % NEARS] = jnp.dot(
            weight[...], tiles(proj, tile, WIDE_LAST), preferred_element_type=F32
        )

    def update(tile, part, slot):
        for row in range(0, bands, ROWS):
            for index in range(WIDE_LAST):
                kinetic = kinetic_tile(kin, tile + index)
                at = (part * WIDE_LAST + index) * LANES
                bufs[slot, row : row + ROWS, at : at + LANES] = moved(
                    current, kinetic, factor, shift, nears.at[part % NEARS], tile + index,
                    row, index,
                )

    ahead(0, 0)

    def body(step, carry):
        slot = lax.rem(step, BUFFERS)

        @pl.when(step >= BUFFERS)
        def _():
            for part in range(split):
                send(step - BUFFERS, part).wait()

        for part in range(parts):
            tile = step * count + part * WIDE_LAST
            if part + 1 < parts:
                ahead(tile + WIDE_LAST, part + 1)
            else:
                ahead(jnp.minimum(tile + WIDE_LAST, (steps - 1) * count), 0)
            update(tile, part, slot)
            if (part + 1) * WIDE_LAST * LANES % piece == 0:
                send(step, (part + 1) * WIDE_LAST * LANES // piece - 1).start()
        return carry

    lax.fori_loop(0, steps, body, 0)
    for step in range(max(0, steps - BUFFERS), steps):
        for part in range(split):
            send(step, part).wait()


VM = pl.BlockSpec(memory_space=pltpu.VMEM)
SM = pl.BlockSpec(memory_space=pltpu.SMEM)
HB = pl.BlockSpec(memory_space=pltpu.HBM)


def params(mib):
    return pltpu.CompilerParams(vmem_limit_bytes=mib * MIB)


def swap(value, axis, mask):
    count = lax.axis_size(axis)
    return lax.ppermute(value, axis, [(i, i ^ mask) for i in range(count)])


def masks_direct(count, first):
    return [mask for mask in (first, 2 * first, 3 * first) if mask < count]


def local(
    wave_coeffs, projectors, miller_index, occupations, species_map, proj_counts, onsite_base
):
    bands, plane = wave_coeffs.shape
    slots = projectors.shape[0]
    half = slots // 2
    bands_all = bands * lax.axis_size("gy")
    core = (lax.axis_index("gx") % 2).astype(jnp.int32).reshape(1)
    rows = bands + ROWS
    chunk_first = min(CHUNK_FIRST, plane // 2)
    chunk_middle = min(CHUNK_MIDDLE, plane // 4)
    chunk_last = min(CHUNK_LAST, plane // 4)
    chunk_factor = min(2048, plane // 4)
    def partial_out(kind):
        return (pltpu.VMEM((rows, half), F32), pltpu.VMEM((rows, half), kind))

    stay = functools.partial(pltpu.with_memory_space_constraint, memory_space=pltpu.HBM)
    count = plane // LANES
    flight = max(2, FLIGHT_BYTES // (2 * (bands + slots) * chunk_first))
    band_tiles = pltpu.VMEM((count, bands, LANES), BF16)
    current, proj, kin, live, base, occ, own, other = pl.pallas_call(
        functools.partial(first_kernel, chunk_first, flight),
        out_shape=(
            band_tiles,
            pltpu.VMEM((count, slots, LANES), BF16),
            pltpu.VMEM((PMAX, plane), F32),
            pltpu.VMEM((PMAX, half), F32),
            pltpu.VMEM((PMAX, half), F32),
            pltpu.VMEM((bands, LANES), F32),
        )
        + partial_out(F32),
        in_specs=[SM] + [HB] * 7,
        out_specs=[VM] * 8,
        scratch_shapes=[
            pltpu.VMEM((flight, bands, chunk_first), BF16),
            pltpu.VMEM((flight, slots, chunk_first), BF16),
        ]
        + [pltpu.VMEM((bands, slots), F32)]
        + [pltpu.VMEM((bands, LANES), F32)] * 2
        + [
            pltpu.VMEM(miller_index.shape, jnp.int32),
            pltpu.VMEM((1, bands), F32),
            pltpu.VMEM(onsite_base.shape, F32),
            pltpu.SMEM(species_map.shape, jnp.int32),
            pltpu.SMEM(proj_counts.shape, jnp.int32),
            pltpu.SemaphoreType.DMA((2, flight)),
            pltpu.SemaphoreType.DMA((5,)),
        ],
        compiler_params=params(12),
    )(
        core, stay(wave_coeffs), stay(projectors), stay(miller_index),
        stay(occupations.reshape(1, bands)), stay(onsite_base), stay(species_map),
        stay(proj_counts),
    )
    for turn in range(ITERS):
        came = swap(other, "gx", 1)
        first = 2
        while True:
            total, sent = pl.pallas_call(
                pair_kernel,
                out_shape=partial_out(F32 if turn + 1 < ITERS else BF16),
                in_specs=[VM, VM],
                out_specs=[VM, VM],
                compiler_params=params(4),
            )(own, came)
            arrived = [swap(sent, "gx", m) for m in masks_direct(lax.axis_size("gx"), first)]
            first *= 4
            if first >= lax.axis_size("gx"):
                break
            own = total
            came = sum(part.astype(F32) for part in arrived)
        masked, density, sums = pl.pallas_call(
            functools.partial(density_kernel, len(arrived)),
            out_shape=(
                pltpu.VMEM((bands, half), F32),
                pltpu.VMEM((PMAX, half), F32),
                pltpu.VMEM((ROWS, bands), F32),
            ),
            in_specs=[VM] * (3 + len(arrived)),
            out_specs=[VM] * 3,
            compiler_params=params(10),
        )(total, *arrived, live, occ)
        others = [swap(density, "gy", m) for m in masks_direct(lax.axis_size("gy"), 1)]
        first = 4
        while first < lax.axis_size("gy"):
            density = density + sum(others)
            others = [swap(density, "gy", m) for m in masks_direct(lax.axis_size("gy"), first)]
            first *= 4
        factor_steps = plane // chunk_factor
        turning = factor_steps * SHARE // 16
        begun, scale, band_kin, norm_inv, done = pl.pallas_call(
            functools.partial(factor_kernel, chunk_factor, 0, turning),
            out_shape=(pltpu.VMEM(wave_coeffs.shape, F32),)
            + (pltpu.VMEM((bands, LANES), F32),) * 3
            + (pltpu.VMEM((PMAX, LANES), F32),),
            in_specs=[VM, VM],
            out_specs=[VM] * 5,
            compiler_params=params(4),
            cost_estimate=pl.CostEstimate(
                flops=12 * bands * plane, bytes_accessed=4 * bands * plane, transcendentals=0
            ),
        )(kin, sums)
        mine = pl.pallas_call(
            functools.partial(weight_kernel, len(others), bands_all),
            out_shape=pltpu.VMEM((bands, half + LANES), BF16),
            in_specs=[VM] * (5 + len(others)),
            out_specs=VM,
            scratch_shapes=[pltpu.VMEM((half, half), F32)],
            compiler_params=params(6),
        )(density, *others, masked, live, base, done)
        theirs = swap(mine, "gx", 1)
        factor = pl.pallas_call(
            functools.partial(factor_rest_kernel, chunk_factor, turning, factor_steps),
            out_shape=pltpu.VMEM(wave_coeffs.shape, F32),
            in_specs=[VM] * 4,
            out_specs=VM,
            input_output_aliases={0: 0},
            compiler_params=params(4),
            cost_estimate=pl.CostEstimate(
                flops=12 * bands * plane, bytes_accessed=4 * bands * plane, transcendentals=0
            ),
        )(begun, kin, scale, mine)
        held = (core, mine, theirs, band_kin, norm_inv, current, proj, kin, factor)
        gathered = [
            pltpu.VMEM((bands, slots), BF16),
            pltpu.VMEM((bands, LANES), F32),
        ]
        if turn + 1 < ITERS:
            current, own, other = pl.pallas_call(
                functools.partial(middle_kernel, chunk_middle),
                out_shape=(band_tiles,)
                + partial_out(F32 if turn + 2 < ITERS else BF16),
                in_specs=[SM] + [VM] * 8,
                out_specs=[VM] * 3,
                scratch_shapes=gathered
                + [pltpu.VMEM((bands, slots), F32)]
                + [pltpu.VMEM((bands, LANES), F32)] * 2
                + [pltpu.VMEM((bands, chunk_middle), F32)] * 2
                + [pltpu.VMEM((chunk_middle // LANES, bands, LANES), BF16)] * 2,
                compiler_params=params(13),
            )(*held)
    return pl.pallas_call(
        functools.partial(last_kernel, chunk_last),
        out_shape=jax.ShapeDtypeStruct(wave_coeffs.shape, F32),
        in_specs=[SM] + [VM] * 8,
        out_specs=HB,
        scratch_shapes=gathered
        + [pltpu.VMEM((NEARS, bands, WIDE_LAST * LANES), F32)]
        + [pltpu.VMEM((BUFFERS, bands, chunk_last), F32), pltpu.SemaphoreType.DMA((BUFFERS, SPLIT))],
        compiler_params=params(11),
    )(*held)


def solution(mesh):
    placed = (P("gy", "gx"), P(None, "gx"), P(None, "gx"), P("gy"), P(), P(), P())
    return jax.shard_map(
        local, mesh=mesh, in_specs=placed, out_specs=P("gy", "gx"), check_vma=False
    )
```
